256 devices in a mesh: dom: 16 (over z, core), grp: 16 (over y, x).
Axes of the slice: x: 4, y: 4, z: 8, core: 2. Of those that a mesh axis runs over, the one named last changes fastest.
Arguments:
- node_latent: bfloat16 [262144, 128], P(('dom', 'grp')), may hold values from -6 to 6
- node_tangent: bfloat16 [262144, 128], P(('dom', 'grp')), may hold values from -6 to 6
- edge_latent: bfloat16 [1048576, 128], P(('dom', 'grp')), may hold values from -6 to 6
- node_counts: int32 [256], P(('dom', 'grp')), may hold values from 512 to 1024, as said below
- edge_counts: int32 [256], P(('dom', 'grp')), may hold values from 2048 to 4096, as said below
- send_lists: int32 [256, 4, 128], P(('dom', 'grp')), may hold values from 0 to 1023, as said below
- edge_source: int32 [256, 4096], P(('dom', 'grp')), may hold values from 0 to 1535, as said below
- edge_target: int32 [256, 4096], P(('dom', 'grp')), may hold values from 0 to 1023, as said below
- coarse_owner: int32 [256, 1024], P(('dom', 'grp')), may hold values from 0 to 511
- coarse_source: int32 [8192, 8], P(('dom', 'grp')), may hold values from 0 to 1535, as said below
- edge_first: bfloat16 [384, 128], replicated, may hold values from -0.3125 to 0.3125
- edge_second: bfloat16 [128, 128], replicated, may hold values from -0.5 to 0.5
- node_first: bfloat16 [256, 128], replicated, may hold values from -0.375 to 0.375
- node_second: bfloat16 [128, 128], replicated, may hold values from -0.5 to 0.5
- message_first: bfloat16 [256, 128], replicated, may hold values from -0.375 to 0.375
- message_second: bfloat16 [128, 128], replicated, may hold values from -0.5 to 0.5
- coarse_first: bfloat16 [256, 128], replicated, may hold values from -0.375 to 0.375
- coarse_second: bfloat16 [128, 128], replicated, may hold values from -0.5 to 0.5
- prolong_first: bfloat16 [256, 128], replicated, may hold values from -0.375 to 0.375
- prolong_second: bfloat16 [128, 128], replicated, may hold values from -0.5 to 0.5
Outputs:
- node_output: bfloat16 [262144, 128], P(('dom', 'grp'))
- tangent_output: bfloat16 [262144, 128], P(('dom', 'grp'))
The draws below stay inside these ranges and needn't reach their ends.
Inputs may be any that keep to these rules, and one draw needn't show every extreme that they name: node_counts[p] is at least half of 1024; some partition has all 1024 slots valid. edge_counts[p] is at least half of 4096; some partition has all 4096 slots valid. `send_lists`: every entry is a valid node row of its own partition (below node_counts[p]). `edge_source`: every entry is either a valid node row of the partition (below node_counts[p]) or a halo row 1024 + r with r < 512. `edge_target`: every entry is a valid node row of the partition. `coarse_source`: entries below 32 * 16 name nodes of row d-1, entries from 2 * 32 * 16 on name nodes of row d+1, the others nodes of row d itself.
All inputs are finite; a program needn't handle non-finite values.
Results may differ from the reference program's by a relative error of at most 0.012.
Values may be sent and summed in bfloat16 or wider, within the bound.
A program may use at most 64 MiB of HBM per device.

```python
import jax
import jax.numpy as jnp
from jax import lax

L = 128
NF_DEV = 1024
E_DEV = 4096
HALO = 128
NC_DEV = 32
KC = 8
PARTS_SIZE = 256
NF = 262144
E = 1048576
NC = 8192
N_DOM = 16
N_GRP = 16


def count_table(key, salt, most):
    drawn = jax.random.randint(jax.random.fold_in(key, salt), (PARTS_SIZE,), most // 2, most + 1)
    chosen = jax.random.randint(jax.random.fold_in(key, salt + 1), (), 0, PARTS_SIZE)
    return jnp.where(jnp.arange(PARTS_SIZE) == chosen, most, drawn).astype(jnp.int32)


def draw_node_counts(key, part):
    return count_table(key, 11, NF_DEV)


def draw_edge_counts(key, part):
    return count_table(key, 31, E_DEV)


def draw_send_lists(key, part):
    nodes = count_table(key, 11, NF_DEV)
    return jax.random.randint(jax.random.fold_in(key, 51), (PARTS_SIZE, 4, HALO), 0, nodes[:, None, None]).astype(jnp.int32)


def draw_edge_source(key, part):
    nodes = count_table(key, 11, NF_DEV)[:, None]
    picked = jax.random.randint(jax.random.fold_in(key, 61), (PARTS_SIZE, E_DEV), 0, nodes + 4 * HALO)
    return jnp.where(picked < nodes, picked, picked - nodes + NF_DEV).astype(jnp.int32)


def draw_edge_target(key, part):
    nodes = count_table(key, 11, NF_DEV)[:, None]
    return jax.random.randint(jax.random.fold_in(key, 71), (PARTS_SIZE, E_DEV), 0, nodes).astype(jnp.int32)


def draw_coarse_source(key, part):
    row_nodes = NC_DEV * N_GRP
    within = jax.random.randint(jax.random.fold_in(key, 81), (NC, KC), 0, row_nodes)
    outside = jax.random.randint(jax.random.fold_in(key, 82), (NC, KC), 0, 4) == 0
    upper = jax.random.randint(jax.random.fold_in(key, 83), (NC, KC), 0, 2)
    return jnp.where(outside, within + 2 * row_nodes * upper, within + row_nodes).astype(jnp.int32)


def place_ends(result, rng, smallest, largest):
    shape = result.shape
    index_at = [jax.random.randint(jax.random.fold_in(rng, axis), (), 0, shape[axis]) for axis in range(len(shape))]
    result = result.at[tuple(index_at)].set(smallest)
    longest = shape.index(max(shape))
    index_at[longest] = (index_at[longest] + 1) % shape[longest]
    return result.at[tuple(index_at)].set(largest)


def block_levels(key, dims, split, low, largest):
    level, own = 1.0, jax.random.fold_in(key, 6)
    for axis_at, shards_of in split:
        steps = jnp.exp(jax.random.uniform(jax.random.fold_in(own, axis_at), (shards_of,), jnp.float32, low / len(split), largest / len(split)))
        level = level * jnp.repeat(steps, dims[axis_at] // shards_of).reshape([-1 if axis == axis_at else 1 for axis in range(len(dims))])
    return level


def scatter_about(stream_key, dims, width, limit, shards=(), kind=jnp.bfloat16):
    values = width * jax.random.normal(stream_key, dims, jnp.float32)
    if shards:
        values = values * block_levels(stream_key, dims, shards, -0.22, 0.18)
    return jnp.clip(values, -limit, limit).astype(kind)


def setup_inputs(seed: int = 0) -> dict:
    seeds = jax.random.split(jax.random.key(seed), 21)
    node_latent = scatter_about(seeds[0], (NF, L), 1.0, 6.0, ((0, 256),))
    node_tangent = scatter_about(seeds[1], (NF, L), 1.0, 6.0, ((0, 256),))
    edge_latent = scatter_about(seeds[2], (E, L), 1.0, 6.0, ((0, 256),))
    node_counts = draw_node_counts(jax.random.fold_in(seeds[20], 71), 0)
    edge_counts = draw_edge_counts(jax.random.fold_in(seeds[20], 71), 0)
    send_lists = draw_send_lists(jax.random.fold_in(seeds[20], 71), 0)
    edge_source = draw_edge_source(jax.random.fold_in(seeds[20], 71), 0)
    edge_target = draw_edge_target(jax.random.fold_in(seeds[20], 71), 0)
    coarse_owner = place_ends(jax.random.randint(seeds[8], (PARTS_SIZE, NF_DEV), 0, NC_DEV * N_GRP), jax.random.fold_in(seeds[8], 1), 0, (NC_DEV * N_GRP) - 1).astype(jnp.int32)
    coarse_source = draw_coarse_source(jax.random.fold_in(seeds[20], 71), 0)
    edge_first = scatter_about(seeds[10], (3 * L, L), (3 * L) ** -0.5, 0.3125)
    edge_second = scatter_about(seeds[11], (L, L), L ** -0.5, 0.5)
    node_first = scatter_about(seeds[12], (2 * L, L), (2 * L) ** -0.5, 0.375)
    node_second = scatter_about(seeds[13], (L, L), L ** -0.5, 0.5)
    message_first = scatter_about(seeds[14], (2 * L, L), (2 * L) ** -0.5, 0.375)
    message_second = scatter_about(seeds[15], (L, L), L ** -0.5, 0.5)
    coarse_first = scatter_about(seeds[16], (2 * L, L), (2 * L) ** -0.5, 0.375)
    coarse_second = scatter_about(seeds[17], (L, L), L ** -0.5, 0.5)
    prolong_first = scatter_about(seeds[18], (2 * L, L), (2 * L) ** -0.5, 0.375)
    prolong_second = scatter_about(seeds[19], (L, L), L ** -0.5, 0.5)
    return {"node_latent": node_latent, "node_tangent": node_tangent, "edge_latent": edge_latent, "node_counts": node_counts, "edge_counts": edge_counts, "send_lists": send_lists, "edge_source": edge_source, "edge_target": edge_target, "coarse_owner": coarse_owner, "coarse_source": coarse_source, "edge_first": edge_first, "edge_second": edge_second, "node_first": node_first, "node_second": node_second, "message_first": message_first, "message_second": message_second, "coarse_first": coarse_first, "coarse_second": coarse_second, "prolong_first": prolong_first, "prolong_second": prolong_second}


def layer_norm(value):
    centred = value - lax.optimization_barrier(jnp.mean(value, axis=-1, keepdims=True))
    spread = lax.optimization_barrier(jnp.mean(centred * centred, axis=-1, keepdims=True))
    return centred * lax.rsqrt(spread + 1e-05)

def perceptron(inputs, first, second):
    hidden = jax.nn.silu(jnp.dot(inputs, first, preferred_element_type=jnp.float32)).astype(jnp.bfloat16)
    return jnp.dot(hidden, second, preferred_element_type=jnp.float32)

def edge_update(edges, source, target, first, second):
    joined = jnp.concatenate([edges, source, target], axis=-1)
    return (edges.astype(jnp.float32) + layer_norm(perceptron(joined, first, second))).astype(jnp.bfloat16)

def node_update(nodes, other, first, second):
    joined = jnp.concatenate([nodes, other], axis=-1)
    return (nodes.astype(jnp.float32) + layer_norm(perceptron(joined, first, second))).astype(jnp.bfloat16)

def coarse_update(table, sources, mine, weights):
    message_first, message_second, coarse_first, coarse_second = weights
    senders = table[sources]
    receivers = jnp.broadcast_to(mine[:, None, :], senders.shape)
    joined = jnp.concatenate([senders, receivers], axis=-1).reshape(-1, 2 * senders.shape[-1])
    terms = perceptron(joined, message_first, message_second).reshape(senders.shape)
    message = lax.optimization_barrier(jnp.sum(terms, axis=1)).astype(jnp.bfloat16)
    joined = jnp.concatenate([mine, message], axis=-1)
    return layer_norm(perceptron(joined, coarse_first, coarse_second)).astype(jnp.bfloat16)

def from_lower(block, axis):
    empty = jnp.zeros_like(lax.slice_in_dim(block, 0, 1, axis=axis))
    return jnp.concatenate([empty, lax.slice_in_dim(block, 0, block.shape[axis] - 1, axis=axis)], axis=axis)

def from_upper(block, axis):
    empty = jnp.zeros_like(lax.slice_in_dim(block, 0, 1, axis=axis))
    return jnp.concatenate([lax.slice_in_dim(block, 1, block.shape[axis], axis=axis), empty], axis=axis)

def reference(node_latent, node_tangent, edge_latent, node_counts, edge_counts, send_lists, edge_source, edge_target, coarse_owner, coarse_source, edge_first, edge_second, node_first, node_second, message_first, message_second, coarse_first, coarse_second, prolong_first, prolong_second):
    paired = jnp.concatenate([node_latent, node_tangent], axis=1).reshape(N_DOM, N_GRP, NF_DEV, 2 * L)
    lists = send_lists.reshape(N_DOM, N_GRP, 4 * HALO)
    sent = jax.vmap(jax.vmap(lambda rows, picks: rows[picks]))(paired, lists).reshape(N_DOM, N_GRP, 4, HALO, 2 * L)
    halo = jnp.stack([from_lower(sent[:, :, 0], 0), from_upper(sent[:, :, 1], 0), from_lower(sent[:, :, 2], 1), from_upper(sent[:, :, 3], 1)], axis=2)
    halo = halo.reshape(N_DOM * N_GRP, 4 * HALO, 2 * L)
    local = paired.reshape(N_DOM * N_GRP, NF_DEV, 2 * L)
    tables = jnp.concatenate([local, halo], axis=1)

    def fine_part(items):
        table, edges, source, target, edge_total = items
        sender = table[source]
        receiver = table[target]
        edge_new, edge_tan = jax.jvp(lambda a, b, c: edge_update(a, b, c, edge_first, edge_second), (edges, sender[:, :L], receiver[:, :L]), (jnp.zeros_like(edges), sender[:, L:], receiver[:, L:]))
        live = (jnp.arange(E_DEV) < edge_total)[:, None]
        agg = jax.ops.segment_sum(jnp.where(live, edge_new.astype(jnp.float32), 0.0), target, num_segments=NF_DEV).astype(jnp.bfloat16)
        agg_tan = jax.ops.segment_sum(jnp.where(live, edge_tan.astype(jnp.float32), 0.0), target, num_segments=NF_DEV).astype(jnp.bfloat16)
        nodes = table[:NF_DEV]
        first, first_tan = jax.jvp(lambda a, b: node_update(a, b, node_first, node_second), (nodes[:, :L], agg), (nodes[:, L:], agg_tan))
        return jnp.concatenate([first, first_tan], axis=1)
    firsts = lax.map(fine_part, (tables, edge_latent.reshape(N_DOM * N_GRP, E_DEV, L), edge_source, edge_target, edge_counts))
    valid = (jnp.arange(NF_DEV)[None, :] < node_counts[:, None])[:, :, None]
    masked = jnp.where(valid, firsts.astype(jnp.float32), 0.0).reshape(N_DOM, N_GRP * NF_DEV, 2 * L)
    owners = coarse_owner.reshape(N_DOM, N_GRP * NF_DEV)
    sums = jax.vmap(lambda values, keys: jax.ops.segment_sum(values, keys, num_segments=NC_DEV * N_GRP))(masked, owners)
    coarse = sums.astype(jnp.bfloat16)
    rows3 = jnp.concatenate([from_lower(coarse, 0), coarse, from_upper(coarse, 0)], axis=1)
    sources = coarse_source.reshape(N_DOM, NC_DEV * N_GRP, KC)
    weights = (message_first, message_second, coarse_first, coarse_second)

    def coarse_row(table, mine, row_sources):
        updated, updated_tan = jax.jvp(lambda a, b: coarse_update(a, row_sources, b, weights), (table[:, :L], mine[:, :L]), (table[:, L:], mine[:, L:]))
        return jnp.concatenate([updated, updated_tan], axis=1)
    updated = jax.vmap(coarse_row)(rows3, coarse, sources)
    pulled = jax.vmap(lambda rows, keys: rows[keys])(updated, owners).reshape(N_DOM * N_GRP, NF_DEV, 2 * L)

    def final_part(items):
        first, brought = items
        final, final_tan = jax.jvp(lambda a, b: node_update(a, b, prolong_first, prolong_second), (first[:, :L], brought[:, :L]), (first[:, L:], brought[:, L:]))
        return jnp.concatenate([final, final_tan], axis=1)
    finals = lax.map(final_part, (firsts, pulled))
    finals = jnp.where(valid, finals, jnp.zeros_like(finals)).reshape(N_DOM * N_GRP * NF_DEV, 2 * L)
    return (finals[:, :L], finals[:, L:])
```

```python
import functools

import jax
import jax.numpy as jnp
from jax import lax
from jax.experimental import pallas as pl
from jax.experimental.pallas import tpu as pltpu
from jax.sharding import PartitionSpec as P

F32, BF16, I32, I16 = jnp.float32, jnp.bfloat16, jnp.int32, jnp.int16
MESH = pl.DeviceIdType.MESH
L = 128
LANES = 128


def dot(a, b):
    return jnp.dot(a, b, preferred_element_type=F32)


def twice(w):
    w = w.astype(F32)
    z = jnp.zeros_like(w)
    both = jnp.concatenate([jnp.concatenate([w, z], 1), jnp.concatenate([z, w], 1)], 0)
    return both.astype(BF16)


def centred(w):
    w = w.astype(F32)
    return w - jnp.mean(w, axis=-1, keepdims=True)


def swish_pair(pre):
    v, vt = pre[:, :L], pre[:, L:]
    gate = 1.0 / (1.0 + jnp.exp(-v))
    h = v * gate
    ht = vt * (gate + h * (1.0 - gate))
    return jnp.concatenate([h.astype(BF16), ht.astype(BF16)], 1)


def norm_pair(value, mean):
    c, ct = value[:, :L], value[:, L:]
    stats = dot(jnp.concatenate([(c * c).astype(BF16), (c * ct).astype(BF16)], 1), mean)
    r = lax.rsqrt(stats[:, :L] + 1e-5)
    y = c * r
    return y, r * ct - y * (r * r * stats[:, L:])


def column(row, kind):
    return jnp.transpose(jnp.broadcast_to(row, (LANES, LANES))).astype(kind)


def residual(base, y):
    return (base.astype(F32) + y).astype(BF16)


def ring_offsets(ny, nx):
    near = lambda a, n: min(a, n - a)
    pairs = [(a, b) for a in range(ny) for b in range(nx) if (a, b) != (0, 0)]
    return sorted(pairs, key=lambda p: (near(p[0], ny) + near(p[1], nx), p))


def layer_kernel(
    sizes,
    node_count, edge_count,
    latent, tangent, edges_hbm, lists, source, target, owner, coarse_source,
    edge_first, edge_second, node_first, node_second, message_first, message_second, coarse_first, coarse_second,
    first_out, updated_out,
    edges, local, halo_out, halo_in, table, columns, onehot, pick, pre, acc, weights, part, arrived, rows3, node_pair,
    load_sem, halo_send, halo_recv, rs_send, rs_recv, ag_send, ag_recv, side_send, side_recv, fin_send, fin_recv,
):
    n_dom, n_grp, ny, nx = sizes
    slots, rim, edge_slots, own = latent.shape[0], lists.shape[2], source.shape[1], coarse_source.shape[0]
    halo_rows, row_nodes = 4 * rim, own * n_grp
    block = onehot.shape[0]
    blocks = edge_slots // block
    d, g = lax.axis_index("dom"), lax.axis_index("grp")
    y, x = g // nx, g % nx
    offsets = ring_offsets(ny, nx)
    ahead = [((y + a) % ny) * nx + (x + b) % nx for a, b in offsets]
    behind = [((y + ny - a) % ny) * nx + (x + nx - b) % nx for a, b in offsets]
    sides = [(d < n_dom - 1, (d + 1, g)), (d > 0, (d - 1, g)), (g < n_grp - 1, (d, g + 1)), (g > 0, (d, g - 1))]
    origins = [d > 0, d < n_dom - 1, g > 0, g < n_grp - 1]

    def remote(src, dst, send, recv, to):
        return pltpu.make_async_remote_copy(src_ref=src, dst_ref=dst, send_sem=send, recv_sem=recv, device_id=to, device_id_type=MESH)

    load = pltpu.make_async_copy(edges_hbm, edges, load_sem)
    load.start()
    barrier = pltpu.get_barrier_semaphore()
    for k in ahead:
        pl.semaphore_signal(barrier, inc=1, device_id=(d, k), device_id_type=MESH)
    for there, to in sides[:2]:
        @pl.when(there)
        def _():
            pl.semaphore_signal(barrier, inc=1, device_id=to, device_id_type=MESH)

    lanes = lax.broadcasted_iota(I32, (LANES, LANES), 1).astype(I16)
    one, zero = jnp.ones((LANES, LANES), BF16), jnp.zeros((LANES, LANES), BF16)

    def spread(ref, row, col, count, col_at):
        for j in range(count):
            ref[row : row + LANES, col + j * LANES : col + (j + 1) * LANES] = jnp.where(
                col_at == lanes + jnp.array(j * LANES, I16), one, zero
            )

    local[:, :L] = latent[...]
    local[:, L:] = tangent[...]
    for b in range(4):
        spread(onehot, b * rim, 0, slots // LANES, column(lists[0, b : b + 1, :], I16))
    halo_out[...] = dot(onehot[:halo_rows, :slots], local[...]).astype(BF16).reshape(halo_out.shape)

    weights[0] = twice(edge_first[L : 2 * L, :])
    weights[1] = twice(edge_first[2 * L : 3 * L, :])
    weights[2] = twice(centred(edge_second[...]))
    weights[3] = twice(jnp.full((L, L), 1.0 / L, F32))
    mean = weights.at[3]

    for b, (there, to) in enumerate(sides):
        @pl.when(jnp.logical_not(origins[b]))
        def _():
            halo_in[b] = jnp.zeros(halo_in.shape[1:], BF16)

    pl.semaphore_wait(barrier, len(ahead) + jnp.where(d > 0, 1, 0) + jnp.where(d < n_dom - 1, 1, 0))
    halo_copies = [remote(halo_out.at[b], halo_in.at[b], halo_send.at[b], halo_recv.at[b], to) for b, (_, to) in enumerate(sides)]
    for b, (there, _) in enumerate(sides):
        @pl.when(there)
        def _():
            halo_copies[b].start()

    table[:slots, :] = dot(local[...], weights[0]).astype(BF16)
    table[slots : 2 * slots, :] = dot(local[...], weights[1]).astype(BF16)
    load.wait()

    def gather_local(i, _):
        at = pl.multiple_of(i * block, block)
        for q in range(block // LANES):
            here = pl.multiple_of(at + q * LANES, LANES)
            s = column(source[0:1, pl.ds(here, LANES)], I16)
            t = column(target[0:1, pl.ds(here, LANES)], I16)
            columns[pl.ds(here, LANES), :] = s
            spread(onehot, q * LANES, 0, slots // LANES, s)
            spread(onehot, q * LANES, slots, slots // LANES, t)
        out = dot(onehot[...], table[: 2 * slots, :])
        pre[pl.ds(at, block), :L] = out[:, :L] + dot(edges[pl.ds(at, block), :], edge_first[:L, :])
        pre[pl.ds(at, block), L:] = out[:, L:]
        return 0

    lax.fori_loop(0, blocks, gather_local, 0)

    for b, there in enumerate(origins):
        @pl.when(there)
        def _():
            halo_copies[b].wait_recv()
    table[2 * slots :, :] = dot(halo_in[...].reshape(halo_rows, 2 * L), weights[0]).astype(BF16)
    acc[...] = jnp.zeros_like(acc)
    total = edge_count[0]
    rows_at = lax.broadcasted_iota(I32, (LANES, block), 0).astype(I16)
    one_b, zero_b = jnp.ones((LANES, block), BF16), jnp.zeros((LANES, block), BF16)

    def edge_block(i, _):
        at = pl.multiple_of(i * block, block)
        for q in range(block // LANES):
            s = columns[pl.ds(pl.multiple_of(at + q * LANES, LANES), LANES), :]
            spread(onehot, q * LANES, 0, halo_rows // LANES, s - jnp.array(slots, I16))
        hidden = swish_pair(pre[pl.ds(at, block), :] + dot(onehot[:, :halo_rows], table[2 * slots :, :]))
        up, up_tan = norm_pair(dot(hidden, weights[2]), mean[...])
        pair = jnp.concatenate([residual(edges[pl.ds(at, block), :], up), up_tan.astype(BF16)], 1)
        ids = at + lax.broadcasted_iota(I32, (1, block), 1)
        live = jnp.where(ids < total, target[0:1, pl.ds(at, block)], -1)
        live = jnp.broadcast_to(live, (LANES, block)).astype(I16)
        for j in range(slots // LANES):
            pick[j * LANES : (j + 1) * LANES, :] = jnp.where(live == rows_at + jnp.array(j * LANES, I16), one_b, zero_b)
        acc[...] += dot(pick[...], pair)
        return 0

    lax.fori_loop(0, blocks, edge_block, 0)

    weights[0] = twice(node_first[:L, :])
    weights[1] = twice(node_first[L:, :])
    weights[2] = twice(centred(node_second[...]))
    hidden = swish_pair(dot(local[...], weights[0]) + dot(acc[...].astype(BF16), weights[1]))
    up, up_tan = norm_pair(dot(hidden, weights[2]), mean[...])
    node_pair[:, :L] = residual(latent[...], up)
    node_pair[:, L:] = residual(tangent[...], up_tan)
    first_out[...] = node_pair[...]

    ids = lax.broadcasted_iota(I32, (1, slots), 1)
    live = jnp.where(ids < node_count[0], owner[...], -1)
    live = jnp.broadcast_to(live, (LANES, slots)).astype(I16)
    rows_n = lax.broadcasted_iota(I32, (LANES, slots), 0).astype(I16)
    one_n, zero_n = jnp.ones((LANES, slots), BF16), jnp.zeros((LANES, slots), BF16)
    for j in range(row_nodes // LANES):
        onehot[j * LANES : (j + 1) * LANES, :slots] = jnp.where(live == rows_n + jnp.array(j * LANES, I16), one_n, zero_n)
    part[...] = dot(onehot[:row_nodes, :slots], node_pair[...]).astype(BF16).reshape(part.shape)

    n = len(offsets)
    rs = [remote(part.at[ahead[m]], arrived.at[m], rs_send.at[m], rs_recv.at[m], (d, ahead[m])) for m in range(n)]
    for m in reversed(range(n)):
        rs[m].start()
    weights[0] = twice(message_first[:L, :])
    weights[1] = twice(message_first[L:, :])
    weights[2] = twice(message_second[...])
    weights[4] = twice(coarse_first[:L, :])
    weights[5] = twice(coarse_first[L:, :])
    weights[6] = twice(centred(coarse_second[...]))
    for j in range(coarse_source.shape[1]):
        ids = lax.broadcasted_iota(I32, (own, 3 * row_nodes), 1)
        onehot[j * own : (j + 1) * own, : 3 * row_nodes] = jnp.where(coarse_source[:, j : j + 1] == ids, 1.0, 0.0).astype(BF16)
    for beyond, slot in ((d == 0, 0), (d == n_dom - 1, 2)):
        @pl.when(beyond)
        def _():
            rows3[slot] = jnp.zeros(rows3.shape[1:], BF16)

    mine = part[g].astype(F32)
    for m in range(n):
        rs[m].wait_recv()
        mine = mine + arrived[m].astype(F32)
    mine = mine.astype(BF16)
    rows3[1, g] = mine

    ag = [remote(rows3.at[1, g], rows3.at[1, g], ag_send.at[m], ag_recv.at[m], (d, ahead[m])) for m in range(n)]
    for m in reversed(range(n)):
        ag[m].start()

    def passed_on(k, m):
        up = remote(rows3.at[1, k], rows3.at[0, k], side_send.at[0, m], side_recv.at[0, m], (d + 1, g))
        down = remote(rows3.at[1, k], rows3.at[2, k], side_send.at[1, m], side_recv.at[1, m], (d - 1, g))
        return up, down

    forwards = [passed_on(g, n)] + [passed_on(behind[m], m) for m in range(n)]
    for m in range(-1, n):
        if m >= 0:
            remote(rows3.at[1, behind[m]], rows3.at[1, behind[m]], ag_send.at[m], ag_recv.at[m], (d, ahead[m])).wait_recv()
        up, down = forwards[m + 1]
        @pl.when(d < n_dom - 1)
        def _():
            up.start()
        @pl.when(d > 0)
        def _():
            down.start()
    senders = dot(onehot[: own * 8, row_nodes : 2 * row_nodes], rows3[1].reshape(row_nodes, 2 * L))
    receiver = dot(mine, weights[1])
    for m in range(n + 1):
        k = g if m == 0 else behind[m - 1]
        i = n if m == 0 else m - 1
        @pl.when(d > 0)
        def _():
            remote(rows3.at[1, k], rows3.at[0, k], side_send.at[0, i], side_recv.at[0, i], (d + 1, g)).wait_recv()
        @pl.when(d < n_dom - 1)
        def _():
            remote(rows3.at[1, k], rows3.at[2, k], side_send.at[1, i], side_recv.at[1, i], (d - 1, g)).wait_recv()
    senders = senders + dot(onehot[: own * 8, :row_nodes], rows3[0].reshape(row_nodes, 2 * L))
    senders = senders + dot(onehot[: own * 8, 2 * row_nodes : 3 * row_nodes], rows3[2].reshape(row_nodes, 2 * L))
    to_all = jnp.concatenate([receiver] * 8, 0)
    hidden = swish_pair(dot(senders.astype(BF16), weights[0]) + to_all)
    terms = dot(hidden, weights[2])
    message = terms[:own]
    for j in range(1, 8):
        message = message + terms[j * own : (j + 1) * own]
    hidden = swish_pair(dot(mine, weights[4]) + dot(message.astype(BF16), weights[5]))
    up, up_tan = norm_pair(dot(hidden, weights[6]), mean[...])
    updated_out[g] = jnp.concatenate([up.astype(BF16), up_tan.astype(BF16)], 1)
    fin = [remote(updated_out.at[g], updated_out.at[g], fin_send.at[m], fin_recv.at[m], (d, ahead[m])) for m in range(n)]
    for m in reversed(range(n)):
        fin[m].start()

    for b, (there, _) in enumerate(sides):
        @pl.when(there)
        def _():
            halo_copies[b].wait_send()
    for m in range(n):
        rs[m].wait_send()
        ag[m].wait_send()
    for up, down in forwards:
        @pl.when(d < n_dom - 1)
        def _():
            up.wait_send()
        @pl.when(d > 0)
        def _():
            down.wait_send()
    for m in range(n):
        fin[m].wait_send()
        remote(updated_out.at[behind[m]], updated_out.at[behind[m]], fin_send.at[m], fin_recv.at[m], (d, ahead[m])).wait_recv()


def final_kernel(node_count, first, updated, owner, prolong_first, prolong_second, node_output, tangent_output, onehot):
    slots, row_nodes = first.shape[0], updated.shape[0]
    lanes = lax.broadcasted_iota(I32, (LANES, LANES), 1).astype(I16)
    one, zero = jnp.ones((LANES, LANES), BF16), jnp.zeros((LANES, LANES), BF16)
    for q in range(slots // LANES):
        at = column(owner[0:1, q * LANES : (q + 1) * LANES], I16)
        for j in range(row_nodes // LANES):
            onehot[q * LANES : (q + 1) * LANES, j * LANES : (j + 1) * LANES] = jnp.where(at == lanes + jnp.array(j * LANES, I16), one, zero)
    brought = dot(onehot[...], updated[...]).astype(BF16)
    mean = twice(jnp.full((L, L), 1.0 / L, F32))
    pair = first[...]
    hidden = swish_pair(dot(pair, twice(prolong_first[:L, :])) + dot(brought, twice(prolong_first[L:, :])))
    up, up_tan = norm_pair(dot(hidden, twice(centred(prolong_second[...]))), mean)
    valid = lax.broadcasted_iota(I32, (slots, L), 0) < node_count[0]
    node_output[...] = jnp.where(valid, pair[:, :L].astype(F32) + up, 0.0).astype(BF16)
    tangent_output[...] = jnp.where(valid, pair[:, L:].astype(F32) + up_tan, 0.0).astype(BF16)


def per_device(
    sizes,
    node_latent, node_tangent, edge_latent, node_counts, edge_counts, send_lists, edge_source, edge_target, coarse_owner, coarse_source,
    edge_first, edge_second, node_first, node_second, message_first, message_second, coarse_first, coarse_second, prolong_first, prolong_second,
):
    n_dom, n_grp, ny, nx = sizes
    slots, edge_slots, rim, own = node_latent.shape[0], edge_latent.shape[0], send_lists.shape[2], coarse_source.shape[0]
    block = 1024
    vmem = pl.BlockSpec(memory_space=pltpu.VMEM)
    smem = pl.BlockSpec(memory_space=pltpu.SMEM)
    others = n_grp - 1
    dma = pltpu.SemaphoreType.DMA
    first, updated = pl.pallas_call(
        functools.partial(layer_kernel, sizes),
        out_shape=(jax.ShapeDtypeStruct((slots, 2 * L), BF16), jax.ShapeDtypeStruct((n_grp, own, 2 * L), BF16)),
        in_specs=[smem, smem, vmem, vmem, pl.BlockSpec(memory_space=pl.ANY)] + [vmem] * 13,
        out_specs=(vmem, vmem),
        scratch_shapes=[
            pltpu.VMEM((edge_slots, L), BF16),
            pltpu.VMEM((slots, 2 * L), BF16),
            pltpu.VMEM((4, rim, 2 * L), BF16),
            pltpu.VMEM((4, rim, 2 * L), BF16),
            pltpu.VMEM((2 * slots + 4 * rim, 2 * L), BF16),
            pltpu.VMEM((edge_slots, LANES), I16),
            pltpu.VMEM((block, 2 * slots), BF16),
            pltpu.VMEM((slots, block), BF16),
            pltpu.VMEM((edge_slots, 2 * L), F32),
            pltpu.VMEM((slots, 2 * L), F32),
            pltpu.VMEM((7, 2 * L, 2 * L), BF16),
            pltpu.VMEM((n_grp, own, 2 * L), BF16),
            pltpu.VMEM((others, own, 2 * L), BF16),
            pltpu.VMEM((3, n_grp, own, 2 * L), BF16),
            pltpu.VMEM((slots, 2 * L), BF16),
            dma(()), dma((4,)), dma((4,)), dma((others,)), dma((others,)), dma((others,)), dma((others,)),
            dma((2, n_grp)), dma((2, n_grp)), dma((others,)), dma((others,)),
        ],
        compiler_params=pltpu.CompilerParams(collective_id=0, has_side_effects=True, vmem_limit_bytes=56 << 20),
    )(
        node_counts, edge_counts, node_latent, node_tangent, edge_latent, send_lists, edge_source, edge_target, coarse_owner, coarse_source,
        edge_first, edge_second, node_first, node_second, message_first, message_second, coarse_first, coarse_second,
    )
    out = jax.ShapeDtypeStruct((slots, L), BF16)
    return pl.pallas_call(
        final_kernel,
        out_shape=(out, out),
        in_specs=[smem] + [vmem] * 5,
        out_specs=(vmem, vmem),
        scratch_shapes=[pltpu.VMEM((slots, own * n_grp), BF16)],
    )(node_counts, first, updated.reshape(n_grp * own, 2 * L), coarse_owner, prolong_first, prolong_second)


def solution(mesh):
    n_dom, n_grp = mesh.shape["dom"], mesh.shape["grp"]
    nx = 4 if n_grp % 4 == 0 and n_grp > 4 else 2
    both = ("dom", "grp")
    rows = P(both, None)
    in_specs = (rows, rows, rows, P(both), P(both), P(both, None, None), rows, rows, rows, rows) + (P(),) * 10
    return jax.shard_map(
        functools.partial(per_device, (n_dom, n_grp, n_grp // nx, nx)),
        mesh=mesh, in_specs=in_specs, out_specs=(rows, rows), check_vma=False,
    )
```

```python
import functools

import jax
import jax.numpy as jnp
from jax import lax
from jax.experimental import pallas as pl
from jax.experimental.pallas import tpu as pltpu
from jax.sharding import PartitionSpec as P

F32, BF16, I32, I16 = jnp.float32, jnp.bfloat16, jnp.int32, jnp.int16
MESH = pl.DeviceIdType.MESH
L = 128
LANES = 128
BLOCK = 1024
NAMES = (
    "node_latent", "node_tangent", "edge_latent", "send_lists", "edge_source", "edge_target",
    "coarse_owner", "coarse_source", "edge_first", "edge_second", "node_first", "node_second", "message_first", "message_second",
    "coarse_first", "coarse_second", "prolong_first", "prolong_second",
)


def dot(a, b):
    return jnp.dot(a, b, preferred_element_type=F32)


def twice(w):
    w = w.astype(F32)
    z = jnp.zeros_like(w)
    both = jnp.concatenate([jnp.concatenate([w, z], 1), jnp.concatenate([z, w], 1)], 0)
    return both.astype(BF16)


def centred(w):
    w = w.astype(F32)
    return w - jnp.mean(w, axis=-1, keepdims=True)


def swish_pair(pre):
    v, vt = pre[:, :L], pre[:, L:]
    gate = 1.0 / (1.0 + jnp.exp(-v))
    h = v * gate
    ht = vt * (gate + h * (1.0 - gate))
    return jnp.concatenate([h.astype(BF16), ht.astype(BF16)], 1)


def norm_pair(value, mean):
    c, ct = value[:, :L], value[:, L:]
    stats = dot(jnp.concatenate([(c * c).astype(BF16), (c * ct).astype(BF16)], 1), mean)
    r = lax.rsqrt(stats[:, :L] + 1e-5)
    y = c * r
    return y, r * ct - y * (r * r * stats[:, L:])


def column(row):
    return jnp.transpose(jnp.broadcast_to(row, (LANES, LANES))).astype(I16)


def iota(shape, axis):
    return lax.broadcasted_iota(I32, shape, axis).astype(I16)


def chosen(hit):
    return jnp.where(hit, jnp.ones(hit.shape, BF16), jnp.zeros(hit.shape, BF16))


def picks(col, count, start=0):
    return chosen(jnp.concatenate([col] * (count // LANES), 1) == iota((col.shape[0], count), 1) + jnp.array(start, I16))


def picks_down(row, count, start=0):
    shape = (count, row.shape[1])
    return chosen(jnp.broadcast_to(row, shape).astype(I16) == iota(shape, 0) + jnp.array(start, I16))


def residual(base, y):
    return (base.astype(F32) + y).astype(BF16)


def ring_offsets(ny, nx):
    near = lambda a, n: min(a, n - a)
    pairs = [(a, b) for a in range(ny) for b in range(nx) if (a, b) != (0, 0)]
    return sorted(pairs, key=lambda p: (near(p[0], ny) + near(p[1], nx), p))


def layer_kernel(sizes, *refs):
    n_dom, n_grp, ny, nx = sizes
    node_count, edge_count = refs[0][0], refs[1][0]
    hbm = dict(zip(NAMES, refs[2:20]))
    (
        node_output, tangent_output,
        local, edges, lists, source, target, owner, coarse_source,
        edge_first, edge_second, node_first, node_second, message_first, message_second, coarse_first, coarse_second, prolong_first, prolong_second,
        halo_out, halo_in, table, columns, pre, pairs, picked, picked_senders, base, weights, part, arrived, rows3, updated, turned, agg,
        load_sem, halo_send, halo_recv, rs_send, rs_recv, ag_send, ag_recv, side_send, side_recv, fin_send, fin_recv,
    ) = refs[20:]
    slots, rim, edge_slots, own, fan = local.shape[0], lists.shape[2], source.shape[1], coarse_source.shape[1], coarse_source.shape[0]
    halo_rows, row_nodes = 4 * rim, own * n_grp
    blocks = edge_slots // BLOCK
    d, g = lax.axis_index("dom"), lax.axis_index("grp")
    y, x = g // nx, g % nx
    offsets = ring_offsets(ny, nx)
    n = len(offsets)
    ahead = [((y + a) % ny) * nx + (x + b) % nx for a, b in offsets]
    behind = [((y + ny - a) % ny) * nx + (x + nx - b) % nx for a, b in offsets]
    sides = [(d < n_dom - 1, (d + 1, g)), (d > 0, (d - 1, g)), (g < n_grp - 1, (d, g + 1)), (g > 0, (d, g - 1))]
    origins = [d > 0, d < n_dom - 1, g > 0, g < n_grp - 1]

    def remote(src, dst, send, recv, to):
        return pltpu.make_async_remote_copy(src_ref=src, dst_ref=dst, send_sem=send, recv_sem=recv, device_id=to, device_id_type=MESH)

    def all_of(ref, sem):
        pltpu.make_async_copy(ref, ref, sem).wait()

    barrier = pltpu.get_barrier_semaphore()
    for k in ahead:
        pl.semaphore_signal(barrier, inc=1, device_id=(d, k), device_id_type=MESH)
    for there, to in sides[:2]:
        @pl.when(there)
        def _():
            pl.semaphore_signal(barrier, inc=1, device_id=to, device_id_type=MESH)

    places = {
        "send_lists": lists, "node_latent": local.at[:, :L], "node_tangent": local.at[:, L:], "edge_first": edge_first,
        "edge_source": source, "edge_target": target, "edge_latent": edges, "edge_second": edge_second,
        "node_first": node_first, "node_second": node_second, "coarse_owner": owner,
        "coarse_source": coarse_source, "message_first": message_first, "message_second": message_second,
        "coarse_first": coarse_first, "coarse_second": coarse_second, "prolong_first": prolong_first, "prolong_second": prolong_second,
    }
    groups = (
        ("send_lists", "node_latent", "node_tangent", "edge_first"),
        ("edge_source", "edge_target", "edge_latent", "edge_second"),
        NAMES[6:8] + NAMES[10:],
    )
    loads = [[pltpu.make_async_copy(hbm[name], places[name], load_sem.at[i]) for name in group] for i, group in enumerate(groups)]
    for group in loads:
        for copy in group:
            copy.start()

    def need(i):
        for copy in loads[i]:
            copy.wait()

    mean = weights.at[3]
    weights[3] = twice(jnp.full((L, L), 1.0 / L, F32))
    need(0)
    sent = jnp.concatenate([column(lists[0, b : b + 1, :]) for b in range(4)], 0)
    halo_out[...] = dot(picks(sent, slots), local[...]).astype(BF16).reshape(halo_out.shape)
    weights[0] = twice(edge_first[L : 2 * L, :])
    weights[1] = twice(edge_first[2 * L : 3 * L, :])
    table[:slots, :] = dot(local[...], weights[0]).astype(BF16)
    table[slots : 2 * slots, :] = dot(local[...], weights[1]).astype(BF16)
    need(1)
    weights[2] = twice(centred(edge_second[...]))

    def index_columns(ref, at):
        parts = [column(ref[0:1, pl.ds(pl.multiple_of(at + q * LANES, LANES), LANES)]) for q in range(BLOCK // LANES)]
        return jnp.concatenate(parts, 0)

    def gathered(at, with_halo):
        s, t = index_columns(source, at), index_columns(target, at)
        if not with_halo:
            columns[pl.ds(at, BLOCK), :] = s
        hot = [picks(s, slots), picks(t, slots)] + ([picks(s, halo_rows, slots)] if with_halo else [])
        rows = dot(jnp.concatenate(hot, 1), table[: 2 * slots + (halo_rows if with_halo else 0), :])
        return jnp.concatenate([rows[:, :L] + dot(edges[pl.ds(at, BLOCK), :], edge_first[:L, :]), rows[:, L:]], 1)

    def edge_pair(at, with_halo):
        value = pre[pl.ds(at, BLOCK), :]
        if with_halo:
            value = value + dot(picks(columns[pl.ds(at, BLOCK), :], halo_rows, slots), table[2 * slots :, :])
        up, up_tan = norm_pair(dot(swish_pair(value), weights[2]), mean[...])
        return jnp.concatenate([residual(edges[pl.ds(at, BLOCK), :], up), up_tan.astype(BF16)], 1)

    halo_copies = [remote(halo_out.at[b], halo_in.at[b], halo_send.at[b], halo_recv.at[b], to) for b, (_, to) in enumerate(sides)]

    def ahead_of_halo(i, _):
        at = pl.multiple_of(i * BLOCK, BLOCK)
        pre[pl.ds(at, BLOCK), :] = gathered(at, False)
        return 0

    early = blocks // 2
    for b in range(4):
        @pl.when(jnp.logical_not(origins[b]))
        def _():
            halo_in[b] = jnp.zeros(halo_in.shape[1:], BF16)

    pl.semaphore_wait(barrier, n + jnp.where(d > 0, 1, 0) + jnp.where(d < n_dom - 1, 1, 0))
    for b, (there, _) in enumerate(sides):
        @pl.when(there)
        def _():
            halo_copies[b].start()
    lax.fori_loop(0, early, ahead_of_halo, 0)
    for b, there in enumerate(origins):
        @pl.when(there)
        def _():
            halo_copies[b].wait_recv()
    table[2 * slots :, :] = dot(halo_in[...].reshape(halo_rows, 2 * L), weights[0]).astype(BF16)

    def both_stages(i, _):
        at = pl.multiple_of(i * BLOCK, BLOCK)
        before = pl.multiple_of(at - early * BLOCK, BLOCK)
        rows = gathered(at, True)
        pairs[pl.ds(before, BLOCK), :] = edge_pair(before, True)
        pre[pl.ds(at, BLOCK), :] = rows
        return 0

    def last_stage(i, _):
        at = pl.multiple_of(i * BLOCK, BLOCK)
        pairs[pl.ds(at, BLOCK), :] = edge_pair(at, False)
        return 0

    lax.fori_loop(early, blocks, both_stages, 0)
    lax.fori_loop(early, blocks, last_stage, 0)

    need(2)
    weights[0] = twice(node_first[:L, :])
    weights[1] = twice(node_first[L:, :])
    weights[2] = twice(centred(node_second[...]))
    live = jnp.where(lax.broadcasted_iota(I32, (1, edge_slots), 1) < edge_count, target[...], -1)
    first = local
    half = slots // 2

    def summed(h, _):
        at = pl.multiple_of(h * half, half)
        agg[pl.ds(at, half), :] = dot(picks_down(live - at, half), pairs[...]).astype(BF16)
        return 0

    lax.fori_loop(0, 2, summed, 0)
    hidden = swish_pair(dot(local[...], weights[0]) + dot(agg[...], weights[1]))
    up, up_tan = norm_pair(dot(hidden, weights[2]), mean[...])
    first[...] = jnp.concatenate([residual(local[:, :L], up), residual(local[:, L:], up_tan)], 1)
    live = jnp.where(lax.broadcasted_iota(I32, (1, slots), 1) < node_count, owner[...], -1)
    part[...] = dot(picks_down(live, row_nodes), first[...]).astype(BF16).reshape(part.shape)

    rs = [remote(part.at[ahead[m]], arrived.at[m], rs_send, rs_recv, (d, ahead[m])) for m in range(n)]
    for m in reversed(range(n)):
        rs[m].start()
    weights[0] = twice(message_first[:L, :])
    weights[1] = twice(message_first[L:, :])
    weights[2] = twice(message_second[...])
    weights[4] = twice(coarse_first[:L, :])
    weights[5] = twice(coarse_first[L:, :])
    weights[6] = twice(centred(coarse_second[...]))
    weights[7] = twice(prolong_first[:L, :])
    weights[8] = twice(prolong_first[L:, :])
    weights[9] = twice(centred(prolong_second[...]))
    turned[...] = jnp.zeros_like(turned)
    turned[:fan, :own] = coarse_source[...]
    senders_at = jnp.transpose(turned[...])
    for j in range(fan):
        at = jnp.broadcast_to(senders_at[:own, j : j + 1], (own, LANES)).astype(I16)
        picked_senders[j * own : (j + 1) * own, :] = picks(at, 3 * row_nodes)
    for beyond, slot in ((d == 0, 0), (d == n_dom - 1, 2)):
        @pl.when(beyond)
        def _():
            rows3[slot] = jnp.zeros(rows3.shape[1:], BF16)

    mine = part[g].astype(F32)
    all_of(arrived, rs_recv)
    for m in range(n):
        mine = mine + arrived[m].astype(F32)
    mine = mine.astype(BF16)
    rows3[1, g] = mine

    ag = [remote(rows3.at[1, g], rows3.at[1, g], ag_send, ag_recv.at[m], (d, ahead[m])) for m in range(n)]
    for m in reversed(range(n)):
        ag[m].start()

    def passed_on(k):
        up = remote(rows3.at[1, k], rows3.at[0, k], side_send.at[0], side_recv.at[0], (d + 1, g))
        down = remote(rows3.at[1, k], rows3.at[2, k], side_send.at[1], side_recv.at[1], (d - 1, g))
        return up, down

    forwards = [passed_on(behind[m]) for m in range(n)] + [passed_on(g)]

    def forward(m):
        up, down = forwards[m]
        @pl.when(d < n_dom - 1)
        def _():
            up.start()
        @pl.when(d > 0)
        def _():
            down.start()

    forward(n)
    for q in range(slots // LANES):
        picked[q * LANES : (q + 1) * LANES, :] = picks(column(owner[0:1, q * LANES : (q + 1) * LANES]), row_nodes)
    base[...] = dot(first[...], weights[7])
    for m in range(n):
        remote(rows3.at[1, behind[m]], rows3.at[1, behind[m]], ag_send, ag_recv.at[m], (d, ahead[m])).wait_recv()
        forward(m)
    senders = dot(picked_senders[:, row_nodes : 2 * row_nodes], rows3[1].reshape(row_nodes, 2 * L))
    receiver = dot(mine, weights[1])
    @pl.when(d > 0)
    def _():
        all_of(rows3.at[0], side_recv.at[0])
    @pl.when(d < n_dom - 1)
    def _():
        all_of(rows3.at[2], side_recv.at[1])
    senders = senders + dot(picked_senders[:, :row_nodes], rows3[0].reshape(row_nodes, 2 * L))
    senders = senders + dot(picked_senders[:, 2 * row_nodes :], rows3[2].reshape(row_nodes, 2 * L))
    hidden = swish_pair(dot(senders.astype(BF16), weights[0]) + jnp.concatenate([receiver] * fan, 0))
    terms = dot(hidden, weights[2])
    message = terms[:own]
    for j in range(1, fan):
        message = message + terms[j * own : (j + 1) * own]
    hidden = swish_pair(dot(mine, weights[4]) + dot(message.astype(BF16), weights[5]))
    up, up_tan = norm_pair(dot(hidden, weights[6]), mean[...])
    updated[g] = jnp.concatenate([up.astype(BF16), up_tan.astype(BF16)], 1)
    fin = [remote(updated.at[g], updated.at[g], fin_send, fin_recv, (d, ahead[m])) for m in range(n)]
    for m in reversed(range(n)):
        fin[m].start()

    for b, (there, _) in enumerate(sides):
        @pl.when(there)
        def _():
            halo_copies[b].wait_send()
    all_of(arrived, rs_send)
    all_of(arrived, ag_send)
    @pl.when(d < n_dom - 1)
    def _():
        all_of(rows3.at[0], side_send.at[0])
    @pl.when(d > 0)
    def _():
        all_of(rows3.at[2], side_send.at[1])
    all_of(arrived, fin_recv)
    brought = dot(picked[...], updated[...].reshape(row_nodes, 2 * L)).astype(BF16)
    hidden = swish_pair(base[...] + dot(brought, weights[8]))
    up, up_tan = norm_pair(dot(hidden, weights[9]), mean[...])
    valid = lax.broadcasted_iota(I32, (slots, L), 0) < node_count
    node_output[...] = jnp.where(valid, first[:, :L].astype(F32) + up, 0.0).astype(BF16)
    tangent_output[...] = jnp.where(valid, first[:, L:].astype(F32) + up_tan, 0.0).astype(BF16)
    all_of(arrived, fin_send)


def per_device(sizes, *args):
    n_dom, n_grp, ny, nx = sizes
    named = dict(zip(NAMES[:3] + ("node_counts", "edge_counts") + NAMES[3:], args))
    named["coarse_source"] = named["coarse_source"].T
    counts = [named.pop(name) for name in ("node_counts", "edge_counts")]
    shape = {name: a.shape for name, a in named.items()}
    slots, edge_slots, rim = shape["node_latent"][0], shape["edge_latent"][0], shape["send_lists"][2]
    fan, own = shape["coarse_source"]
    row_nodes = n_grp * own
    others = n_grp - 1
    dma = pltpu.SemaphoreType.DMA
    vmem = pltpu.VMEM
    out = jax.ShapeDtypeStruct((slots, L), BF16)
    return pl.pallas_call(
        functools.partial(layer_kernel, sizes),
        out_shape=(out, out),
        in_specs=[pl.BlockSpec(memory_space=pltpu.SMEM)] * 2 + [pl.BlockSpec(memory_space=pltpu.HBM)] * 18,
        out_specs=(pl.BlockSpec(memory_space=vmem),) * 2,
        scratch_shapes=[vmem((slots, 2 * L), BF16), vmem((edge_slots, L), BF16)]
        + [vmem(shape[name], I32) for name in NAMES[3:8]]
        + [vmem(shape[name], BF16) for name in NAMES[8:]]
        + [
            vmem((4, rim, 2 * L), BF16),
            vmem((4, rim, 2 * L), BF16),
            vmem((2 * slots + 4 * rim, 2 * L), BF16),
            vmem((edge_slots // 2, LANES), I16),
            vmem((edge_slots, 2 * L), F32),
            vmem((edge_slots, 2 * L), BF16),
            vmem((slots, row_nodes), BF16),
            vmem((fan * own, 3 * row_nodes), BF16),
            vmem((slots, 2 * L), F32),
            vmem((10, 2 * L, 2 * L), BF16),
            vmem((n_grp, own, 2 * L), BF16),
            vmem((others, own, 2 * L), BF16),
            vmem((3, n_grp, own, 2 * L), BF16),
            vmem((n_grp, own, 2 * L), BF16),
            vmem((LANES, LANES), I32),
            vmem((slots, 2 * L), BF16),
            dma((3,)), dma((4,)), dma((4,)), dma(()), dma(()), dma(()), dma((others,)), dma((2,)), dma((2,)), dma(()), dma(()),
        ],
        compiler_params=pltpu.CompilerParams(collective_id=0, has_side_effects=True, vmem_limit_bytes=VMEM_LIMIT << 20),
    )(*counts, *[pltpu.with_memory_space_constraint(a, pltpu.HBM) for a in named.values()])


VMEM_LIMIT = 40


def solution(mesh):
    n_dom, n_grp = mesh.shape["dom"], mesh.shape["grp"]
    nx = 4 if n_grp % 4 == 0 and n_grp > 4 else 2
    both = ("dom", "grp")
    rows = P(both, None)
    in_specs = (rows, rows, rows, P(both), P(both), P(both, None, None), rows, rows, rows, rows) + (P(),) * 10
    return jax.shard_map(
        functools.partial(per_device, (n_dom, n_grp, n_grp // nx, nx)),
        mesh=mesh, in_specs=in_specs, out_specs=(rows, rows), check_vma=False,
    )
```

```python
import functools

import jax
import jax.numpy as jnp
from jax import lax
from jax.experimental import pallas as pl
from jax.experimental.pallas import tpu as pltpu
from jax.sharding import PartitionSpec as P

F32, BF16, I32, I16 = jnp.float32, jnp.bfloat16, jnp.int32, jnp.int16
MESH = pl.DeviceIdType.MESH
L = 128
LANES = 128
BLOCK = 1024
NAMES = (
    "node_latent", "node_tangent", "edge_latent", "send_lists", "edge_source", "edge_target",
    "coarse_owner", "coarse_source", "edge_first", "edge_second", "node_first", "node_second", "message_first", "message_second",
    "coarse_first", "coarse_second", "prolong_first", "prolong_second",
)


def dot(a, b):
    return jnp.dot(a, b, preferred_element_type=F32)


def twice(w):
    w = w.astype(F32)
    z = jnp.zeros_like(w)
    both = jnp.concatenate([jnp.concatenate([w, z], 1), jnp.concatenate([z, w], 1)], 0)
    return both.astype(BF16)


def centred(w):
    w = w.astype(F32)
    return w - jnp.mean(w, axis=-1, keepdims=True)


def swish_pair(pre):
    v, vt = pre[:, :L], pre[:, L:]
    gate = 1.0 / (1.0 + jnp.exp(-v))
    h = v * gate
    ht = vt * (gate + h * (1.0 - gate))
    return jnp.concatenate([h.astype(BF16), ht.astype(BF16)], 1)


def norm_pair(value, mean):
    c, ct = value[:, :L], value[:, L:]
    stats = dot(jnp.concatenate([(c * c).astype(BF16), (c * ct).astype(BF16)], 1), mean)
    r = lax.rsqrt(stats[:, :L] + 1e-5)
    y = c * r
    return y, r * ct - y * (r * r * stats[:, L:])


def norm_pair_lanes(value):
    c, ct = value[:, :L], value[:, L:]
    r = lax.rsqrt(jnp.mean(c * c, axis=-1, keepdims=True) + 1e-5)
    y = c * r
    return y, r * ct - y * (r * r * jnp.mean(c * ct, axis=-1, keepdims=True))


def column(row):
    return jnp.transpose(jnp.broadcast_to(row, (LANES, LANES))).astype(I16)


def iota(shape, axis):
    return lax.broadcasted_iota(I32, shape, axis).astype(I16)


def chosen(hit):
    return jnp.where(hit, jnp.ones(hit.shape, BF16), jnp.zeros(hit.shape, BF16))


def picks(col, count, start=0):
    return chosen(jnp.concatenate([col] * (count // LANES), 1) == iota((col.shape[0], count), 1) + jnp.array(start, I16))


def picks_down(row, count, start=0):
    shape = (count, row.shape[1])
    return chosen(jnp.broadcast_to(row, shape).astype(I16) == iota(shape, 0) + jnp.array(start, I16))


def residual(base, y):
    return (base.astype(F32) + y).astype(BF16)


def ring_offsets(ny, nx):
    near = lambda a, n: min(a, n - a)
    pairs = [(a, b) for a in range(ny) for b in range(nx) if (a, b) != (0, 0)]
    return sorted(pairs, key=lambda p: (near(p[0], ny) + near(p[1], nx), p))


def layer_kernel(sizes, *refs):
    n_dom, n_grp, ny, nx = sizes
    node_count, edge_count = refs[0][0], refs[1][0]
    hbm = dict(zip(NAMES, refs[2:20]))
    (
        node_output, tangent_output,
        local, edges, lists, source, target, owner, coarse_source,
        edge_first, edge_second, node_first, node_second, message_first, message_second, coarse_first, coarse_second, prolong_first, prolong_second,
        halo_out, halo_in, table, columns, pre, pairs, picked, picked_senders, base, weights, part, arrived, rows3, updated, turned, agg, owners_down, sent,
        load_sem, halo_send, halo_recv, rs_send, rs_recv, ag_send, ag_recv, side_send, side_recv, fin_send, fin_recv,
    ) = refs[20:]
    slots, rim, edge_slots, own, fan = local.shape[0], lists.shape[2], source.shape[1], coarse_source.shape[1], coarse_source.shape[0]
    halo_rows, row_nodes = 4 * rim, own * n_grp
    blocks = edge_slots // BLOCK
    d, g = lax.axis_index("dom"), lax.axis_index("grp")
    y, x = g // nx, g % nx
    offsets = ring_offsets(ny, nx)
    n = len(offsets)
    ahead = [((y + a) % ny) * nx + (x + b) % nx for a, b in offsets]
    behind = [((y + ny - a) % ny) * nx + (x + nx - b) % nx for a, b in offsets]
    sides = [(d < n_dom - 1, (d + 1, g)), (d > 0, (d - 1, g)), (g < n_grp - 1, (d, g + 1)), (g > 0, (d, g - 1))]
    origins = [d > 0, d < n_dom - 1, g > 0, g < n_grp - 1]

    def remote(src, dst, send, recv, to):
        return pltpu.make_async_remote_copy(src_ref=src, dst_ref=dst, send_sem=send, recv_sem=recv, device_id=to, device_id_type=MESH)

    def all_of(ref, sem):
        pltpu.make_async_copy(ref, ref, sem).wait()

    barrier = pltpu.get_barrier_semaphore()
    for k in ahead:
        pl.semaphore_signal(barrier, inc=1, device_id=(d, k), device_id_type=MESH)
    for there, to in sides[:2]:
        @pl.when(there)
        def _():
            pl.semaphore_signal(barrier, inc=1, device_id=to, device_id_type=MESH)

    places = {
        "send_lists": lists, "node_latent": local.at[:, :L], "node_tangent": local.at[:, L:], "edge_first": edge_first,
        "edge_source": source, "edge_target": target, "edge_latent": edges, "edge_second": edge_second,
        "node_first": node_first, "node_second": node_second, "coarse_owner": owner,
        "coarse_source": coarse_source, "message_first": message_first, "message_second": message_second,
        "coarse_first": coarse_first, "coarse_second": coarse_second, "prolong_first": prolong_first, "prolong_second": prolong_second,
    }
    groups = (
        ("node_latent", "node_tangent", "edge_first"),
        ("edge_source", "edge_target", "edge_latent", "edge_second"),
        NAMES[6:8] + NAMES[10:],
        ("send_lists",),
    )
    loads = [[pltpu.make_async_copy(hbm[name], places[name], load_sem.at[i]) for name in group] for i, group in enumerate(groups)]

    def bring(i):
        for copy in loads[i]:
            copy.start()

    def need(i):
        for copy in loads[i]:
            copy.wait()

    bring(3)
    bring(0)

    mean = weights.at[3]
    weights[3] = twice(jnp.full((L, L), 1.0 / L, F32))
    need(3)
    for b in range(4):
        sent[b * rim : (b + 1) * rim, :] = picks(column(lists[0, b : b + 1, :]), slots)
    need(0)
    bring(1)
    bring(2)
    halo_out[...] = dot(sent[...], local[...]).astype(BF16).reshape(halo_out.shape)
    weights[0] = twice(edge_first[L : 2 * L, :])
    weights[1] = twice(edge_first[2 * L : 3 * L, :])
    table[:slots, :] = dot(local[...], weights[0]).astype(BF16)
    table[slots : 2 * slots, :] = dot(local[...], weights[1]).astype(BF16)
    need(1)
    weights[2] = twice(centred(edge_second[...]))

    def index_columns(ref, at):
        parts = [column(ref[0:1, pl.ds(pl.multiple_of(at + q * LANES, LANES), LANES)]) for q in range(BLOCK // LANES)]
        return jnp.concatenate(parts, 0)

    def gathered(at, with_halo):
        s, t = index_columns(source, at), index_columns(target, at)
        if not with_halo:
            columns[pl.ds(at, BLOCK), :] = s
        hot = [picks(s, slots), picks(t, slots)] + ([picks(s, halo_rows, slots)] if with_halo else [])
        rows = dot(jnp.concatenate(hot, 1), table[: 2 * slots + (halo_rows if with_halo else 0), :])
        return jnp.concatenate([rows[:, :L] + dot(edges[pl.ds(at, BLOCK), :], edge_first[:L, :]), rows[:, L:]], 1)

    def edge_pair(at, with_halo):
        value = pre[pl.ds(at, BLOCK), :]
        if with_halo:
            value = value + dot(picks(columns[pl.ds(at, BLOCK), :], halo_rows, slots), table[2 * slots :, :])
        value = dot(swish_pair(value), weights[2])
        up, up_tan = norm_pair_lanes(value) if with_halo else norm_pair(value, mean[...])
        return jnp.concatenate([residual(edges[pl.ds(at, BLOCK), :], up), up_tan.astype(BF16)], 1)

    halo_copies = [remote(halo_out.at[b], halo_in.at[b], halo_send.at[b], halo_recv.at[b], to) for b, (_, to) in enumerate(sides)]

    def ahead_of_halo(i, _):
        at = pl.multiple_of(i * BLOCK, BLOCK)
        pre[pl.ds(at, BLOCK), :] = gathered(at, False)
        return 0

    early = blocks // 2
    for b in range(4):
        @pl.when(jnp.logical_not(origins[b]))
        def _():
            halo_in[b] = jnp.zeros(halo_in.shape[1:], BF16)

    pl.semaphore_wait(barrier, n + jnp.where(d > 0, 1, 0) + jnp.where(d < n_dom - 1, 1, 0))
    for b, (there, _) in enumerate(sides):
        @pl.when(there)
        def _():
            halo_copies[b].start()
    lax.fori_loop(0, early, ahead_of_halo, 0)
    for b, there in enumerate(origins):
        @pl.when(there)
        def _():
            halo_copies[b].wait_recv()
    table[2 * slots :, :] = dot(halo_in[...].reshape(halo_rows, 2 * L), weights[0]).astype(BF16)

    def both_stages(i, _):
        at = pl.multiple_of(i * BLOCK, BLOCK)
        before = pl.multiple_of(at - early * BLOCK, BLOCK)
        rows = gathered(at, True)
        share = row_nodes // early
        to = pl.multiple_of((i - early) * share, share)
        owners_down[pl.ds(to, share), :] = picks_down(kept - to, share)
        pairs[pl.ds(before, BLOCK), :] = edge_pair(before, True)
        pre[pl.ds(at, BLOCK), :] = rows
        return 0

    def last_stage(i, _):
        at = pl.multiple_of(i * BLOCK, BLOCK)
        pairs[pl.ds(at, BLOCK), :] = edge_pair(at, False)
        rows = pl.ds(pl.multiple_of((i - early) * (slots // early), slots // early), slots // early)
        base[rows, :] = dot(local[rows, :], weights[10])
        return 0

    need(2)
    node = owner[...]
    piece = own // 2
    node = lax.rem(lax.div(node, piece), 2) * (row_nodes // 2) + lax.div(node, own) * piece + lax.rem(node, piece)
    kept = jnp.where(lax.broadcasted_iota(I32, (1, slots), 1) < node_count, node, -1)
    weights[10] = twice(node_first[:L, :])
    lax.fori_loop(early, blocks, both_stages, 0)
    lax.fori_loop(early, blocks, last_stage, 0)

    weights[1] = twice(node_first[L:, :])
    weights[2] = twice(centred(node_second[...]))
    live = jnp.where(lax.broadcasted_iota(I32, (1, edge_slots), 1) < edge_count, target[...], -1)
    first = local
    half = slots // 2

    def summed(h, _):
        at = pl.multiple_of(h * half, half)
        agg[pl.ds(at, half), :] = dot(picks_down(live - at, half), pairs[...]).astype(BF16)
        return 0

    lax.fori_loop(0, 2, summed, 0)
    hidden = swish_pair(base[...] + dot(agg[...], weights[1]))
    up, up_tan = norm_pair(dot(hidden, weights[2]), mean[...])
    first[...] = jnp.concatenate([residual(local[:, :L], up), residual(local[:, L:], up_tan)], 1)
    for c in range(2):
        some = slice(c * (row_nodes // 2), (c + 1) * (row_nodes // 2))
        part[c] = dot(owners_down[some, :], first[...]).astype(BF16).reshape(part.shape[1:])
        for m in reversed(range(n)):
            remote(part.at[c, ahead[m]], arrived.at[c, m], rs_send, rs_recv.at[c], (d, ahead[m])).start()
    weights[0] = twice(message_first[:L, :])
    weights[1] = twice(message_first[L:, :])
    weights[4] = twice(coarse_first[:L, :])
    weights[5] = twice(dot(message_second[...], coarse_first[L:, :]))
    weights[6] = twice(centred(coarse_second[...]))
    weights[7] = twice(prolong_first[:L, :])
    weights[8] = twice(prolong_first[L:, :])
    weights[9] = twice(centred(prolong_second[...]))
    turned[...] = jnp.zeros_like(turned)
    turned[:fan, :own] = coarse_source[...]
    senders_at = jnp.transpose(turned[...])
    for j in range(fan):
        at = jnp.broadcast_to(senders_at[:own, j : j + 1], (own, LANES)).astype(I16)
        picked_senders[j * own : (j + 1) * own, :] = picks(at, 3 * row_nodes)
    for beyond, slot in ((d == 0, 0), (d == n_dom - 1, 2)):
        @pl.when(beyond)
        def _():
            rows3[slot] = jnp.zeros(rows3.shape[1:], BF16)

    for c in range(2):
        rows = pl.ds(c * piece, piece)
        all_of(arrived.at[c], rs_recv.at[c])
        total = part[c, g].astype(F32)
        for m in range(n):
            total = total + arrived[c, m].astype(F32)
        rows3[1, g, rows] = total.astype(BF16)
        for m in reversed(range(n)):
            remote(rows3.at[1, g, rows], rows3.at[1, g, rows], ag_send, ag_recv.at[m], (d, ahead[m])).start()
    mine = rows3[1, g]

    def passed_on(k):
        up = remote(rows3.at[1, k], rows3.at[0, k], side_send.at[0], side_recv.at[0], (d + 1, g))
        down = remote(rows3.at[1, k], rows3.at[2, k], side_send.at[1], side_recv.at[1], (d - 1, g))
        return up, down

    forwards = [passed_on(behind[m]) for m in range(n)] + [passed_on(g)]

    def forward(m):
        up, down = forwards[m]
        @pl.when(d < n_dom - 1)
        def _():
            up.start()
        @pl.when(d > 0)
        def _():
            down.start()

    forward(n)
    for q in range(slots // LANES):
        picked[q * LANES : (q + 1) * LANES, :] = picks(column(owner[0:1, q * LANES : (q + 1) * LANES]), row_nodes)
    base[...] = dot(first[...], weights[7])
    for m in range(n):
        remote(rows3.at[1, behind[m]], rows3.at[1, behind[m]], ag_send, ag_recv.at[m], (d, ahead[m])).wait_recv()
        forward(m)
    senders = dot(picked_senders[:, row_nodes : 2 * row_nodes], rows3[1].reshape(row_nodes, 2 * L))
    receiver = dot(mine, weights[1])
    own_part = dot(mine, weights[4])
    @pl.when(d > 0)
    def _():
        all_of(rows3.at[0], side_recv.at[0])
    @pl.when(d < n_dom - 1)
    def _():
        all_of(rows3.at[2], side_recv.at[1])
    senders = senders + dot(picked_senders[:, :row_nodes], rows3[0].reshape(row_nodes, 2 * L))
    senders = senders + dot(picked_senders[:, 2 * row_nodes :], rows3[2].reshape(row_nodes, 2 * L))
    hidden = swish_pair(dot(senders.astype(BF16), weights[0]) + jnp.concatenate([receiver] * fan, 0))
    message = hidden[:own].astype(F32)
    for j in range(1, fan):
        message = message + hidden[j * own : (j + 1) * own].astype(F32)
    hidden = swish_pair(own_part + dot(message.astype(BF16), weights[5]))
    up, up_tan = norm_pair_lanes(dot(hidden, weights[6]))
    updated[g] = jnp.concatenate([up.astype(BF16), up_tan.astype(BF16)], 1)
    fin = [remote(updated.at[g], updated.at[g], fin_send, fin_recv, (d, ahead[m])) for m in range(n)]
    for m in reversed(range(n)):
        fin[m].start()

    for b, (there, _) in enumerate(sides):
        @pl.when(there)
        def _():
            halo_copies[b].wait_send()
    all_of(arrived, rs_send)
    all_of(arrived, ag_send)
    @pl.when(d < n_dom - 1)
    def _():
        all_of(rows3.at[0], side_send.at[0])
    @pl.when(d > 0)
    def _():
        all_of(rows3.at[2], side_send.at[1])
    all_of(arrived, fin_recv)
    brought = dot(updated[...].reshape(row_nodes, 2 * L), weights[8]).astype(BF16)
    hidden = swish_pair(base[...] + dot(picked[...], brought))
    up, up_tan = norm_pair(dot(hidden, weights[9]), mean[...])
    valid = lax.broadcasted_iota(I32, (slots, L), 0) < node_count
    node_output[...] = jnp.where(valid, first[:, :L].astype(F32) + up, 0.0).astype(BF16)
    tangent_output[...] = jnp.where(valid, first[:, L:].astype(F32) + up_tan, 0.0).astype(BF16)
    all_of(arrived, fin_send)


def store_kernel(primal, tan, node_output, tangent_output, sems):
    copies = [pltpu.make_async_copy(primal, node_output, sems.at[0]), pltpu.make_async_copy(tan, tangent_output, sems.at[1])]
    for copy in copies:
        copy.start()
    for copy in copies:
        copy.wait()


def per_device(sizes, *args):
    n_dom, n_grp, ny, nx = sizes
    named = dict(zip(NAMES[:3] + ("node_counts", "edge_counts") + NAMES[3:], args))
    named["coarse_source"] = named["coarse_source"].T
    counts = [named.pop(name) for name in ("node_counts", "edge_counts")]
    shape = {name: a.shape for name, a in named.items()}
    slots, edge_slots, rim = shape["node_latent"][0], shape["edge_latent"][0], shape["send_lists"][2]
    fan, own = shape["coarse_source"]
    row_nodes = n_grp * own
    others = n_grp - 1
    dma = pltpu.SemaphoreType.DMA
    vmem = pltpu.VMEM
    out = jax.ShapeDtypeStruct((slots, L), BF16)
    results = pl.pallas_call(
        functools.partial(layer_kernel, sizes),
        out_shape=(out, out),
        in_specs=[pl.BlockSpec(memory_space=pltpu.SMEM)] * 2 + [pl.BlockSpec(memory_space=pltpu.HBM)] * 18,
        out_specs=(pl.BlockSpec(memory_space=vmem),) * 2,
        scratch_shapes=[vmem((slots, 2 * L), BF16), vmem((edge_slots, L), BF16)]
        + [vmem(shape[name], I32) for name in NAMES[3:8]]
        + [vmem(shape[name], BF16) for name in NAMES[8:]]
        + [
            vmem((4, rim, 2 * L), BF16),
            vmem((4, rim, 2 * L), BF16),
            vmem((2 * slots + 4 * rim, 2 * L), BF16),
            vmem((edge_slots // 2, LANES), I16),
            vmem((edge_slots, 2 * L), F32),
            vmem((edge_slots, 2 * L), BF16),
            vmem((slots, row_nodes), BF16),
            vmem((fan * own, 3 * row_nodes), BF16),
            vmem((slots, 2 * L), F32),
            vmem((11, 2 * L, 2 * L), BF16),
            vmem((2, n_grp, own // 2, 2 * L), BF16),
            vmem((2, others, own // 2, 2 * L), BF16),
            vmem((3, n_grp, own, 2 * L), BF16),
            vmem((n_grp, own, 2 * L), BF16),
            vmem((LANES, LANES), I32),
            vmem((slots, 2 * L), BF16),
            vmem((row_nodes, slots), BF16),
            vmem((4 * rim, slots), BF16),
            dma((4,)), dma((4,)), dma((4,)), dma(()), dma((2,)), dma(()), dma((others,)), dma((2,)), dma((2,)), dma(()), dma(()),
        ],
        compiler_params=pltpu.CompilerParams(collective_id=0, has_side_effects=True, vmem_limit_bytes=VMEM_LIMIT << 20),
    )(*counts, *[pltpu.with_memory_space_constraint(a, pltpu.HBM) for a in named.values()])
    return pl.pallas_call(
        store_kernel,
        out_shape=(out, out),
        in_specs=[pl.BlockSpec(memory_space=pl.ANY)] * 2,
        out_specs=(pl.BlockSpec(memory_space=pltpu.HBM),) * 2,
        scratch_shapes=[dma((2,))],
    )(*[pltpu.with_memory_space_constraint(a, pltpu.VMEM) for a in results])


VMEM_LIMIT = 40


def solution(mesh):
    n_dom, n_grp = mesh.shape["dom"], mesh.shape["grp"]
    nx = 4 if n_grp % 4 == 0 and n_grp > 4 else 2
    both = ("dom", "grp")
    rows = P(both, None)
    in_specs = (rows, rows, rows, P(both), P(both), P(both, None, None), rows, rows, rows, rows) + (P(),) * 10
    return jax.shard_map(
        functools.partial(per_device, (n_dom, n_grp, n_grp // nx, nx)),
        mesh=mesh, in_specs=in_specs, out_specs=(rows, rows), check_vma=False,
    )
```

```python
import functools

import jax
import jax.numpy as jnp
from jax import lax
from jax.experimental import pallas as pl
from jax.experimental.pallas import tpu as pltpu
from jax.sharding import PartitionSpec as P

F32, BF16, I32, I16 = jnp.float32, jnp.bfloat16, jnp.int32, jnp.int16
MESH = pl.DeviceIdType.MESH
L = 128
LANES = 128
BLOCK = 1024
NAMES = (
    "node_latent", "node_tangent", "edge_latent", "send_lists", "edge_source", "edge_target",
    "coarse_owner", "coarse_source", "edge_first", "edge_second", "node_first", "node_second", "message_first", "message_second",
    "coarse_first", "coarse_second", "prolong_first", "prolong_second",
)


def dot(a, b):
    return jnp.dot(a, b, preferred_element_type=F32)


def twice(w):
    w = w.astype(F32)
    z = jnp.zeros_like(w)
    both = jnp.concatenate([jnp.concatenate([w, z], 1), jnp.concatenate([z, w], 1)], 0)
    return both.astype(BF16)


def centred(w):
    w = w.astype(F32)
    return w - jnp.mean(w, axis=-1, keepdims=True)


def swish_pair(pre):
    v, vt = pre[:, :L], pre[:, L:]
    gate = 1.0 / (1.0 + jnp.exp(-v))
    h = v * gate
    ht = vt * (gate + h * (1.0 - gate))
    return jnp.concatenate([h.astype(BF16), ht.astype(BF16)], 1)


def norm_pair(value, mean):
    c, ct = value[:, :L], value[:, L:]
    stats = dot(jnp.concatenate([(c * c).astype(BF16), (c * ct).astype(BF16)], 1), mean)
    r = lax.rsqrt(stats[:, :L] + 1e-5)
    y = c * r
    return y, r * ct - y * (r * r * stats[:, L:])


def norm_pair_lanes(value):
    c, ct = value[:, :L], value[:, L:]
    r = lax.rsqrt(jnp.mean(c * c, axis=-1, keepdims=True) + 1e-5)
    y = c * r
    return y, r * ct - y * (r * r * jnp.mean(c * ct, axis=-1, keepdims=True))


def column(row):
    return jnp.transpose(jnp.broadcast_to(row, (LANES, LANES))).astype(I16)


def iota(shape, axis):
    return lax.broadcasted_iota(I32, shape, axis).astype(I16)


def chosen(hit):
    return jnp.where(hit, jnp.ones(hit.shape, BF16), jnp.zeros(hit.shape, BF16))


def picks(col, count, start=0):
    return chosen(jnp.concatenate([col] * (count // LANES), 1) == iota((col.shape[0], count), 1) + jnp.array(start, I16))


def picks_down(row, count, start=0):
    shape = (count, row.shape[1])
    return chosen(jnp.broadcast_to(row, shape).astype(I16) == iota(shape, 0) + jnp.array(start, I16))


def residual(base, y):
    return (base.astype(F32) + y).astype(BF16)


def ring_offsets(ny, nx):
    near = lambda a, n: min(a, n - a)
    pairs = [(a, b) for a in range(ny) for b in range(nx) if (a, b) != (0, 0)]
    return sorted(pairs, key=lambda p: (near(p[0], ny) + near(p[1], nx), p))


def layer_kernel(sizes, *refs):
    n_dom, n_grp, ny, nx = sizes
    node_count, edge_count = refs[0][0], refs[1][0]
    hbm = dict(zip(NAMES, refs[2:20]))
    (
        node_output, tangent_output,
        local, edges, lists, source, target, owner, coarse_source,
        edge_first, edge_second, node_first, node_second, message_first, message_second, coarse_first, coarse_second, prolong_first, prolong_second,
        halo_out, halo_in, table, columns, pre, pairs, picked, picked_senders, base, weights, part, arrived, rows3, updated, turned, agg, owners_down, sent,
        load_sem, halo_send, halo_recv, rs_send, rs_recv, ag_send, ag_recv, side_send, side_recv, fin_send, fin_recv,
    ) = refs[20:]
    slots, rim, edge_slots, own, fan = local.shape[0], lists.shape[2], source.shape[1], coarse_source.shape[1], coarse_source.shape[0]
    halo_rows, row_nodes = 4 * rim, own * n_grp
    blocks = edge_slots // BLOCK
    d, g = lax.axis_index("dom"), lax.axis_index("grp")
    y, x = g // nx, g % nx
    offsets = ring_offsets(ny, nx)
    n = len(offsets)
    ahead = [((y + a) % ny) * nx + (x + b) % nx for a, b in offsets]
    behind = [((y + ny - a) % ny) * nx + (x + nx - b) % nx for a, b in offsets]
    sides = [(d < n_dom - 1, (d + 1, g)), (d > 0, (d - 1, g)), (g < n_grp - 1, (d, g + 1)), (g > 0, (d, g - 1))]
    origins = [d > 0, d < n_dom - 1, g > 0, g < n_grp - 1]

    def remote(src, dst, send, recv, to):
        return pltpu.make_async_remote_copy(src_ref=src, dst_ref=dst, send_sem=send, recv_sem=recv, device_id=to, device_id_type=MESH)

    def all_of(ref, sem):
        pltpu.make_async_copy(ref, ref, sem).wait()

    barrier = pltpu.get_barrier_semaphore()
    for k in ahead:
        pl.semaphore_signal(barrier, inc=1, device_id=(d, k), device_id_type=MESH)
    for there, to in sides[:2]:
        @pl.when(there)
        def _():
            pl.semaphore_signal(barrier, inc=1, device_id=to, device_id_type=MESH)

    places = {
        "send_lists": lists, "node_latent": local.at[:, :L], "node_tangent": local.at[:, L:], "edge_first": edge_first,
        "edge_source": source, "edge_target": target, "edge_latent": edges, "edge_second": edge_second,
        "node_first": node_first, "node_second": node_second, "coarse_owner": owner,
        "coarse_source": coarse_source, "message_first": message_first, "message_second": message_second,
        "coarse_first": coarse_first, "coarse_second": coarse_second, "prolong_first": prolong_first, "prolong_second": prolong_second,
    }
    groups = (
        ("node_latent", "node_tangent"),
        ("edge_source", "edge_target", "edge_latent", "edge_second"),
        NAMES[6:8] + NAMES[10:],
        ("send_lists", "edge_first"),
    )
    loads = [[pltpu.make_async_copy(hbm[name], places[name], load_sem.at[i]) for name in group] for i, group in enumerate(groups)]

    def bring(i):
        for copy in loads[i]:
            copy.start()

    def need(i):
        for copy in loads[i]:
            copy.wait()

    bring(3)
    bring(0)

    mean = weights.at[3]
    weights[3] = twice(jnp.full((L, L), 1.0 / L, F32))
    need(3)
    for b in range(4):
        sent[b * rim : (b + 1) * rim, :] = picks(column(lists[0, b : b + 1, :]), slots)
    weights[0] = twice(edge_first[L : 2 * L, :])
    weights[1] = twice(edge_first[2 * L : 3 * L, :])
    need(0)
    bring(1)
    bring(2)
    halo_out[...] = dot(sent[...], local[...]).astype(BF16).reshape(halo_out.shape)
    table[:slots, :] = dot(local[...], weights[0]).astype(BF16)
    table[slots : 2 * slots, :] = dot(local[...], weights[1]).astype(BF16)
    need(1)
    weights[2] = twice(centred(edge_second[...]))

    def index_columns(ref, at):
        parts = [column(ref[0:1, pl.ds(pl.multiple_of(at + q * LANES, LANES), LANES)]) for q in range(BLOCK // LANES)]
        return jnp.concatenate(parts, 0)

    def gathered(at, with_halo):
        s, t = index_columns(source, at), index_columns(target, at)
        if not with_halo:
            columns[pl.ds(at, BLOCK), :] = s
        hot = [picks(s, slots), picks(t, slots)] + ([picks(s, halo_rows, slots)] if with_halo else [])
        rows = dot(jnp.concatenate(hot, 1), table[: 2 * slots + (halo_rows if with_halo else 0), :])
        return jnp.concatenate([rows[:, :L] + dot(edges[pl.ds(at, BLOCK), :], edge_first[:L, :]), rows[:, L:]], 1)

    def edge_pair(at, with_halo):
        value = pre[pl.ds(at, BLOCK), :]
        if with_halo:
            value = value + dot(picks(columns[pl.ds(at, BLOCK), :], halo_rows, slots), table[2 * slots :, :])
        value = dot(swish_pair(value), weights[2])
        up, up_tan = norm_pair_lanes(value) if with_halo else norm_pair(value, mean[...])
        return jnp.concatenate([residual(edges[pl.ds(at, BLOCK), :], up), up_tan.astype(BF16)], 1)

    halo_copies = [remote(halo_out.at[b], halo_in.at[b], halo_send.at[b], halo_recv.at[b], to) for b, (_, to) in enumerate(sides)]

    def ahead_of_halo(i, _):
        at = pl.multiple_of(i * BLOCK, BLOCK)
        pre[pl.ds(at, BLOCK), :] = gathered(at, False)
        return 0

    early = blocks // 2
    for b in range(4):
        @pl.when(jnp.logical_not(origins[b]))
        def _():
            halo_in[b] = jnp.zeros(halo_in.shape[1:], BF16)

    pl.semaphore_wait(barrier, n + jnp.where(d > 0, 1, 0) + jnp.where(d < n_dom - 1, 1, 0))
    for b, (there, _) in enumerate(sides):
        @pl.when(there)
        def _():
            halo_copies[b].start()
    lax.fori_loop(0, early, ahead_of_halo, 0)
    for b, there in enumerate(origins):
        @pl.when(there)
        def _():
            halo_copies[b].wait_recv()
    table[2 * slots :, :] = dot(halo_in[...].reshape(halo_rows, 2 * L), weights[0]).astype(BF16)

    def both_stages(i, _):
        at = pl.multiple_of(i * BLOCK, BLOCK)
        before = pl.multiple_of(at - early * BLOCK, BLOCK)
        rows = gathered(at, True)
        share = row_nodes // early
        to = pl.multiple_of((i - early) * share, share)
        owners_down[pl.ds(to, share), :] = picks_down(kept - to, share)
        pairs[pl.ds(before, BLOCK), :] = edge_pair(before, True)
        pre[pl.ds(at, BLOCK), :] = rows
        return 0

    def last_stage(i, _):
        at = pl.multiple_of(i * BLOCK, BLOCK)
        pairs[pl.ds(at, BLOCK), :] = edge_pair(at, False)
        rows = pl.ds(pl.multiple_of((i - early) * (slots // early), slots // early), slots // early)
        base[rows, :] = dot(local[rows, :], weights[10])
        return 0

    need(2)
    node = owner[...]
    piece = own // 2
    node = lax.rem(lax.div(node, piece), 2) * (row_nodes // 2) + lax.div(node, own) * piece + lax.rem(node, piece)
    kept = jnp.where(lax.broadcasted_iota(I32, (1, slots), 1) < node_count, node, -1)
    weights[10] = twice(node_first[:L, :])
    lax.fori_loop(early, blocks, both_stages, 0)
    lax.fori_loop(early, blocks, last_stage, 0)

    weights[1] = twice(node_first[L:, :])
    weights[2] = twice(centred(node_second[...]))
    live = jnp.where(lax.broadcasted_iota(I32, (1, edge_slots), 1) < edge_count, target[...], -1)
    first = local
    half = slots // 2

    def summed(h, _):
        at = pl.multiple_of(h * half, half)
        agg[pl.ds(at, half), :] = dot(picks_down(live - at, half), pairs[...]).astype(BF16)
        return 0

    lax.fori_loop(0, 2, summed, 0)
    hidden = swish_pair(base[...] + dot(agg[...], weights[1]))
    up, up_tan = norm_pair_lanes(dot(hidden, weights[2]))
    first[...] = jnp.concatenate([residual(local[:, :L], up), residual(local[:, L:], up_tan)], 1)
    for c in range(2):
        some = slice(c * (row_nodes // 2), (c + 1) * (row_nodes // 2))
        part[c] = dot(owners_down[some, :], first[...]).astype(BF16).reshape(part.shape[1:])
        for m in reversed(range(n)):
            remote(part.at[c, ahead[m]], arrived.at[c, m], rs_send, rs_recv.at[c], (d, ahead[m])).start()
    weights[0] = twice(message_first[:L, :])
    weights[1] = twice(message_first[L:, :])
    weights[4] = twice(coarse_first[:L, :])
    weights[5] = twice(dot(message_second[...], coarse_first[L:, :]))
    weights[6] = twice(centred(coarse_second[...]))
    weights[7] = twice(prolong_first[:L, :])
    weights[8] = twice(prolong_first[L:, :])
    weights[9] = twice(centred(prolong_second[...]))
    turned[...] = jnp.zeros_like(turned)
    turned[:fan, :own] = coarse_source[...]
    senders_at = jnp.transpose(turned[...])
    for j in range(fan):
        at = jnp.broadcast_to(senders_at[:own, j : j + 1], (own, LANES)).astype(I16)
        picked_senders[j * own : (j + 1) * own, :] = picks(at, 3 * row_nodes)
    for beyond, slot in ((d == 0, 0), (d == n_dom - 1, 2)):
        @pl.when(beyond)
        def _():
            rows3[slot] = jnp.zeros(rows3.shape[1:], BF16)

    for c in range(2):
        rows = pl.ds(c * piece, piece)
        all_of(arrived.at[c], rs_recv.at[c])
        total = part[c, g].astype(F32)
        for m in range(n):
            total = total + arrived[c, m].astype(F32)
        rows3[1, g, rows] = total.astype(BF16)
        for m in (range(n) if c == 1 else reversed(range(n))):
            remote(rows3.at[1, g, rows], rows3.at[1, g, rows], ag_send, ag_recv.at[m], (d, ahead[m])).start()
    mine = rows3[1, g]

    def passed_on(k):
        up = remote(rows3.at[1, k], rows3.at[0, k], side_send.at[0], side_recv.at[0], (d + 1, g))
        down = remote(rows3.at[1, k], rows3.at[2, k], side_send.at[1], side_recv.at[1], (d - 1, g))
        return up, down

    forwards = [passed_on(behind[m]) for m in range(n)] + [passed_on(g)]

    def forward(m):
        up, down = forwards[m]
        @pl.when(d < n_dom - 1)
        def _():
            up.start()
        @pl.when(d > 0)
        def _():
            down.start()

    forward(n)
    for q in range(slots // LANES):
        picked[q * LANES : (q + 1) * LANES, :] = picks(column(owner[0:1, q * LANES : (q + 1) * LANES]), row_nodes)
    base[...] = dot(first[...], weights[7])
    for m in range(n):
        remote(rows3.at[1, behind[m]], rows3.at[1, behind[m]], ag_send, ag_recv.at[m], (d, ahead[m])).wait_recv()
        forward(m)
    senders = dot(picked_senders[:, row_nodes : 2 * row_nodes], rows3[1].reshape(row_nodes, 2 * L))
    receiver = dot(mine, weights[1])
    own_part = dot(mine, weights[4])
    @pl.when(d > 0)
    def _():
        all_of(rows3.at[0], side_recv.at[0])
    @pl.when(d < n_dom - 1)
    def _():
        all_of(rows3.at[2], side_recv.at[1])
    senders = senders + dot(picked_senders[:, :row_nodes], rows3[0].reshape(row_nodes, 2 * L))
    senders = senders + dot(picked_senders[:, 2 * row_nodes :], rows3[2].reshape(row_nodes, 2 * L))
    hidden = swish_pair(dot(senders.astype(BF16), weights[0]) + jnp.concatenate([receiver] * fan, 0))
    message = hidden[:own].astype(F32)
    for j in range(1, fan):
        message = message + hidden[j * own : (j + 1) * own].astype(F32)
    hidden = swish_pair(own_part + dot(message.astype(BF16), weights[5]))
    up, up_tan = norm_pair_lanes(dot(hidden, weights[6]))
    updated[g] = jnp.concatenate([up.astype(BF16), up_tan.astype(BF16)], 1)
    fin = [remote(updated.at[g], updated.at[g], fin_send, fin_recv, (d, ahead[m])) for m in range(n)]
    for m in reversed(range(n)):
        fin[m].start()

    for b, (there, _) in enumerate(sides):
        @pl.when(there)
        def _():
            halo_copies[b].wait_send()
    all_of(arrived, rs_send)
    all_of(arrived, ag_send)
    @pl.when(d < n_dom - 1)
    def _():
        all_of(rows3.at[0], side_send.at[0])
    @pl.when(d > 0)
    def _():
        all_of(rows3.at[2], side_send.at[1])
    all_of(arrived, fin_recv)
    brought = dot(updated[...].reshape(row_nodes, 2 * L), weights[8]).astype(BF16)
    hidden = swish_pair(base[...] + dot(picked[...], brought))
    up, up_tan = norm_pair_lanes(dot(hidden, weights[9]))
    valid = lax.broadcasted_iota(I32, (slots, L), 0) < node_count
    node_output[...] = jnp.where(valid, first[:, :L].astype(F32) + up, 0.0).astype(BF16)
    tangent_output[...] = jnp.where(valid, first[:, L:].astype(F32) + up_tan, 0.0).astype(BF16)
    all_of(arrived, fin_send)


def store_kernel(primal, tan, node_output, tangent_output, sems):
    copies = [pltpu.make_async_copy(primal, node_output, sems.at[0]), pltpu.make_async_copy(tan, tangent_output, sems.at[1])]
    for copy in copies:
        copy.start()
    for copy in copies:
        copy.wait()


def per_device(sizes, *args):
    n_dom, n_grp, ny, nx = sizes
    named = dict(zip(NAMES[:3] + ("node_counts", "edge_counts") + NAMES[3:], args))
    named["coarse_source"] = named["coarse_source"].T
    counts = [named.pop(name) for name in ("node_counts", "edge_counts")]
    shape = {name: a.shape for name, a in named.items()}
    slots, edge_slots, rim = shape["node_latent"][0], shape["edge_latent"][0], shape["send_lists"][2]
    fan, own = shape["coarse_source"]
    row_nodes = n_grp * own
    others = n_grp - 1
    dma = pltpu.SemaphoreType.DMA
    vmem = pltpu.VMEM
    out = jax.ShapeDtypeStruct((slots, L), BF16)
    results = pl.pallas_call(
        functools.partial(layer_kernel, sizes),
        out_shape=(out, out),
        in_specs=[pl.BlockSpec(memory_space=pltpu.SMEM)] * 2 + [pl.BlockSpec(memory_space=pltpu.HBM)] * 18,
        out_specs=(pl.BlockSpec(memory_space=vmem),) * 2,
        scratch_shapes=[vmem((slots, 2 * L), BF16), vmem((edge_slots, L), BF16)]
        + [vmem(shape[name], I32) for name in NAMES[3:8]]
        + [vmem(shape[name], BF16) for name in NAMES[8:]]
        + [
            vmem((4, rim, 2 * L), BF16),
            vmem((4, rim, 2 * L), BF16),
            vmem((2 * slots + 4 * rim, 2 * L), BF16),
            vmem((edge_slots // 2, LANES), I16),
            vmem((edge_slots, 2 * L), F32),
            vmem((edge_slots, 2 * L), BF16),
            vmem((slots, row_nodes), BF16),
            vmem((fan * own, 3 * row_nodes), BF16),
            vmem((slots, 2 * L), F32),
            vmem((11, 2 * L, 2 * L), BF16),
            vmem((2, n_grp, own // 2, 2 * L), BF16),
            vmem((2, others, own // 2, 2 * L), BF16),
            vmem((3, n_grp, own, 2 * L), BF16),
            vmem((n_grp, own, 2 * L), BF16),
            vmem((LANES, LANES), I32),
            vmem((slots, 2 * L), BF16),
            vmem((row_nodes, slots), BF16),
            vmem((4 * rim, slots), BF16),
            dma((4,)), dma((4,)), dma((4,)), dma(()), dma((2,)), dma(()), dma((others,)), dma((2,)), dma((2,)), dma(()), dma(()),
        ],
        compiler_params=pltpu.CompilerParams(collective_id=0, has_side_effects=True, vmem_limit_bytes=VMEM_LIMIT << 20),
    )(*counts, *[pltpu.with_memory_space_constraint(a, pltpu.HBM) for a in named.values()])
    return pl.pallas_call(
        store_kernel,
        out_shape=(out, out),
        in_specs=[pl.BlockSpec(memory_space=pl.ANY)] * 2,
        out_specs=(pl.BlockSpec(memory_space=pltpu.HBM),) * 2,
        scratch_shapes=[dma((2,))],
    )(*[pltpu.with_memory_space_constraint(a, pltpu.VMEM) for a in results])


VMEM_LIMIT = 40


def solution(mesh):
    n_dom, n_grp = mesh.shape["dom"], mesh.shape["grp"]
    nx = 4 if n_grp % 4 == 0 and n_grp > 4 else 2
    both = ("dom", "grp")
    rows = P(both, None)
    in_specs = (rows, rows, rows, P(both), P(both), P(both, None, None), rows, rows, rows, rows) + (P(),) * 10
    return jax.shard_map(
        functools.partial(per_device, (n_dom, n_grp, n_grp // nx, nx)),
        mesh=mesh, in_specs=in_specs, out_specs=(rows, rows), check_vma=False,
    )
```

```python
import functools

import jax
import jax.numpy as jnp
from jax import lax
from jax.experimental import pallas as pl
from jax.experimental.pallas import tpu as pltpu
from jax.sharding import PartitionSpec as P

F32, BF16, I32, I16 = jnp.float32, jnp.bfloat16, jnp.int32, jnp.int16
MESH = pl.DeviceIdType.MESH
L = 128
LANES = 128
BLOCK = 1024
NAMES = (
    "node_latent", "node_tangent", "edge_latent", "send_lists", "edge_source", "edge_target",
    "coarse_owner", "coarse_source", "edge_first", "edge_second", "node_first", "node_second", "message_first", "message_second",
    "coarse_first", "coarse_second", "prolong_first", "prolong_second",
)


def dot(a, b):
    return jnp.dot(a, b, preferred_element_type=F32)


def twice(w):
    w = w.astype(F32)
    z = jnp.zeros_like(w)
    both = jnp.concatenate([jnp.concatenate([w, z], 1), jnp.concatenate([z, w], 1)], 0)
    return both.astype(BF16)


def centred(w):
    w = w.astype(F32)
    return w - jnp.mean(w, axis=-1, keepdims=True)


def swish_pair(pre):
    v, vt = pre[:, :L], pre[:, L:]
    gate = 1.0 / (1.0 + jnp.exp(-v))
    h = v * gate
    ht = vt * (gate + h * (1.0 - gate))
    return jnp.concatenate([h.astype(BF16), ht.astype(BF16)], 1)


def norm_pair(value, mean):
    c, ct = value[:, :L], value[:, L:]
    stats = dot(jnp.concatenate([(c * c).astype(BF16), (c * ct).astype(BF16)], 1), mean)
    r = lax.rsqrt(stats[:, :L] + 1e-5)
    y = c * r
    return y, r * ct - y * (r * r * stats[:, L:])


def norm_pair_lanes(value):
    c, ct = value[:, :L], value[:, L:]
    r = lax.rsqrt(jnp.mean(c * c, axis=-1, keepdims=True) + 1e-5)
    y = c * r
    return y, r * ct - y * (r * r * jnp.mean(c * ct, axis=-1, keepdims=True))


def column(row):
    return jnp.transpose(jnp.broadcast_to(row, (LANES, LANES))).astype(I16)


def iota(shape, axis):
    return lax.broadcasted_iota(I32, shape, axis).astype(I16)


def chosen(hit):
    return jnp.where(hit, jnp.ones(hit.shape, BF16), jnp.zeros(hit.shape, BF16))


def picks(col, count, start=0):
    return chosen(jnp.concatenate([col] * (count // LANES), 1) == iota((col.shape[0], count), 1) + jnp.array(start, I16))


def picks_down(row, count, start=0):
    shape = (count, row.shape[1])
    return chosen(jnp.broadcast_to(row, shape).astype(I16) == iota(shape, 0) + jnp.array(start, I16))


def residual(base, y):
    return (base.astype(F32) + y).astype(BF16)


def ring_offsets(ny, nx):
    near = lambda a, n: min(a, n - a)
    pairs = [(a, b) for a in range(ny) for b in range(nx) if (a, b) != (0, 0)]
    return sorted(pairs, key=lambda p: (near(p[0], ny) + near(p[1], nx), p))


def layer_kernel(sizes, *refs):
    n_dom, n_grp, ny, nx = sizes
    node_count, edge_count = refs[0][0], refs[1][0]
    hbm = dict(zip(NAMES, refs[2:20]))
    (
        node_output, tangent_output,
        local, edges, lists, source, target, owner, coarse_source,
        edge_first, edge_second, node_first, node_second, message_first, message_second, coarse_first, coarse_second, prolong_first, prolong_second,
        halo_out, halo_in, table, columns, pre, pairs, picked, picked_senders, base, weights, part, arrived, rows3, updated, turned, agg, owners_down, sent,
        load_sem, halo_send, halo_recv, rs_send, rs_recv, ag_send, ag_recv, side_send, side_recv, fin_send, fin_recv,
    ) = refs[20:]
    slots, rim, edge_slots, own, fan = local.shape[0], lists.shape[2], source.shape[1], coarse_source.shape[1], coarse_source.shape[0]
    halo_rows, row_nodes = 4 * rim, own * n_grp
    blocks = edge_slots // BLOCK
    d, g = lax.axis_index("dom"), lax.axis_index("grp")
    y, x = g // nx, g % nx
    offsets = ring_offsets(ny, nx)
    n = len(offsets)
    odd = d % 2
    turns = [(a + odd * ((ny - a) % ny - a), b + odd * ((nx - b) % nx - b)) for a, b in offsets]
    ahead = [((y + a) % ny) * nx + (x + b) % nx for a, b in turns]
    behind = [((y + ny - a) % ny) * nx + (x + nx - b) % nx for a, b in turns]
    sides = [(d < n_dom - 1, (d + 1, g)), (d > 0, (d - 1, g)), (g < n_grp - 1, (d, g + 1)), (g > 0, (d, g - 1))]
    origins = [d > 0, d < n_dom - 1, g > 0, g < n_grp - 1]

    def remote(src, dst, send, recv, to):
        return pltpu.make_async_remote_copy(src_ref=src, dst_ref=dst, send_sem=send, recv_sem=recv, device_id=to, device_id_type=MESH)

    def all_of(ref, sem):
        pltpu.make_async_copy(ref, ref, sem).wait()

    barrier = pltpu.get_barrier_semaphore()
    for k in ahead:
        pl.semaphore_signal(barrier, inc=1, device_id=(d, k), device_id_type=MESH)
    for there, to in sides[:2]:
        @pl.when(there)
        def _():
            pl.semaphore_signal(barrier, inc=1, device_id=to, device_id_type=MESH)

    places = {
        "send_lists": lists, "node_latent": local.at[:, :L], "node_tangent": local.at[:, L:], "edge_first": edge_first,
        "edge_source": source, "edge_target": target, "edge_latent": edges, "edge_second": edge_second,
        "node_first": node_first, "node_second": node_second, "coarse_owner": owner,
        "coarse_source": coarse_source, "message_first": message_first, "message_second": message_second,
        "coarse_first": coarse_first, "coarse_second": coarse_second, "prolong_first": prolong_first, "prolong_second": prolong_second,
    }
    groups = (
        ("node_latent", "node_tangent"),
        ("edge_source", "edge_target", "edge_latent", "edge_second"),
        NAMES[6:8] + NAMES[10:],
        ("send_lists", "edge_first"),
    )
    loads = [[pltpu.make_async_copy(hbm[name], places[name], load_sem.at[i]) for name in group] for i, group in enumerate(groups)]

    def bring(i):
        for copy in loads[i]:
            copy.start()

    def need(i):
        for copy in loads[i]:
            copy.wait()

    bring(3)
    bring(0)

    mean = weights.at[3]
    weights[3] = twice(jnp.full((L, L), 1.0 / L, F32))
    need(3)
    for b in range(4):
        sent[b * rim : (b + 1) * rim, :] = picks(column(lists[0, b : b + 1, :]), slots)
    weights[0] = twice(edge_first[L : 2 * L, :])
    weights[1] = twice(edge_first[2 * L : 3 * L, :])
    need(0)
    bring(1)
    bring(2)
    halo_out[...] = dot(sent[...], local[...]).astype(BF16).reshape(halo_out.shape)
    table[:slots, :] = dot(local[...], weights[0]).astype(BF16)
    table[slots : 2 * slots, :] = dot(local[...], weights[1]).astype(BF16)
    need(1)
    weights[2] = twice(centred(edge_second[...]))

    def index_columns(ref, at):
        parts = [column(ref[0:1, pl.ds(pl.multiple_of(at + q * LANES, LANES), LANES)]) for q in range(BLOCK // LANES)]
        return jnp.concatenate(parts, 0)

    def gathered(at, with_halo):
        s, t = index_columns(source, at), index_columns(target, at)
        if not with_halo:
            columns[pl.ds(at, BLOCK), :] = s
        hot = [picks(s, slots), picks(t, slots)] + ([picks(s, halo_rows, slots)] if with_halo else [])
        rows = dot(jnp.concatenate(hot, 1), table[: 2 * slots + (halo_rows if with_halo else 0), :])
        return jnp.concatenate([rows[:, :L] + dot(edges[pl.ds(at, BLOCK), :], edge_first[:L, :]), rows[:, L:]], 1)

    def edge_pair(at, with_halo):
        value = pre[pl.ds(at, BLOCK), :]
        if with_halo:
            value = value + dot(picks(columns[pl.ds(at, BLOCK), :], halo_rows, slots), table[2 * slots :, :])
        value = dot(swish_pair(value), weights[2])
        up, up_tan = norm_pair_lanes(value) if with_halo else norm_pair(value, mean[...])
        return jnp.concatenate([residual(edges[pl.ds(at, BLOCK), :], up), up_tan.astype(BF16)], 1)

    halo_copies = [remote(halo_out.at[b], halo_in.at[b], halo_send.at[b], halo_recv.at[b], to) for b, (_, to) in enumerate(sides)]

    def ahead_of_halo(i, _):
        at = pl.multiple_of(i * BLOCK, BLOCK)
        pre[pl.ds(at, BLOCK), :] = gathered(at, False)
        return 0

    early = blocks // 2
    for b in range(4):
        @pl.when(jnp.logical_not(origins[b]))
        def _():
            halo_in[b] = jnp.zeros(halo_in.shape[1:], BF16)

    pl.semaphore_wait(barrier, n + jnp.where(d > 0, 1, 0) + jnp.where(d < n_dom - 1, 1, 0))
    for b, (there, _) in enumerate(sides):
        @pl.when(there)
        def _():
            halo_copies[b].start()
    lax.fori_loop(0, early, ahead_of_halo, 0)
    for b, there in enumerate(origins):
        @pl.when(there)
        def _():
            halo_copies[b].wait_recv()
    table[2 * slots :, :] = dot(halo_in[...].reshape(halo_rows, 2 * L), weights[0]).astype(BF16)

    def both_stages(i, _):
        at = pl.multiple_of(i * BLOCK, BLOCK)
        before = pl.multiple_of(at - early * BLOCK, BLOCK)
        rows = gathered(at, True)
        share = row_nodes // early
        to = pl.multiple_of((i - early) * share, share)
        owners_down[pl.ds(to, share), :] = picks_down(kept - to, share)
        pairs[pl.ds(before, BLOCK), :] = edge_pair(before, True)
        pre[pl.ds(at, BLOCK), :] = rows
        return 0

    def last_stage(i, _):
        at = pl.multiple_of(i * BLOCK, BLOCK)
        pairs[pl.ds(at, BLOCK), :] = edge_pair(at, False)
        rows = pl.ds(pl.multiple_of((i - early) * (slots // early), slots // early), slots // early)
        base[rows, :] = dot(local[rows, :], weights[10])
        return 0

    need(2)
    node = owner[...]
    piece = own // 2
    node = lax.rem(lax.div(node, piece), 2) * (row_nodes // 2) + lax.div(node, own) * piece + lax.rem(node, piece)
    kept = jnp.where(lax.broadcasted_iota(I32, (1, slots), 1) < node_count, node, -1)
    weights[10] = twice(node_first[:L, :])
    lax.fori_loop(early, blocks, both_stages, 0)
    lax.fori_loop(early, blocks, last_stage, 0)

    weights[1] = twice(node_first[L:, :])
    weights[2] = twice(centred(node_second[...]))
    live = jnp.where(lax.broadcasted_iota(I32, (1, edge_slots), 1) < edge_count, target[...], -1)
    first = local
    half = slots // 2

    def summed(h, _):
        at = pl.multiple_of(h * half, half)
        agg[pl.ds(at, half), :] = dot(picks_down(live - at, half), pairs[...]).astype(BF16)
        return 0

    lax.fori_loop(0, 2, summed, 0)
    hidden = swish_pair(base[...] + dot(agg[...], weights[1]))
    up, up_tan = norm_pair_lanes(dot(hidden, weights[2]))
    first[...] = jnp.concatenate([residual(local[:, :L], up), residual(local[:, L:], up_tan)], 1)
    for c in range(2):
        some = slice(c * (row_nodes // 2), (c + 1) * (row_nodes // 2))
        part[c] = dot(owners_down[some, :], first[...]).astype(BF16).reshape(part.shape[1:])
        for m in reversed(range(n)):
            remote(part.at[c, ahead[m]], arrived.at[c, m], rs_send, rs_recv.at[c], (d, ahead[m])).start()
    weights[0] = twice(message_first[:L, :])
    weights[1] = twice(message_first[L:, :])
    weights[4] = twice(coarse_first[:L, :])
    weights[5] = twice(dot(message_second[...], coarse_first[L:, :]))
    weights[6] = twice(centred(coarse_second[...]))
    weights[7] = twice(prolong_first[:L, :])
    weights[8] = twice(prolong_first[L:, :])
    weights[9] = twice(centred(prolong_second[...]))
    turned[...] = jnp.zeros_like(turned)
    turned[:fan, :own] = coarse_source[...]
    senders_at = jnp.transpose(turned[...])
    for j in range(fan):
        at = jnp.broadcast_to(senders_at[:own, j : j + 1], (own, LANES)).astype(I16)
        picked_senders[j * own : (j + 1) * own, :] = picks(at, 3 * row_nodes)
    for beyond, slot in ((d == 0, 0), (d == n_dom - 1, 2)):
        @pl.when(beyond)
        def _():
            rows3[slot] = jnp.zeros(rows3.shape[1:], BF16)

    for c in range(2):
        rows = pl.ds(c * piece, piece)
        all_of(arrived.at[c], rs_recv.at[c])
        total = part[c, g].astype(F32)
        for m in range(n):
            total = total + arrived[c, m].astype(F32)
        rows3[1, g, rows] = total.astype(BF16)
        for m in (range(n) if c == 1 else reversed(range(n))):
            remote(rows3.at[1, g, rows], rows3.at[1, g, rows], ag_send, ag_recv.at[m], (d, ahead[m])).start()
    mine = rows3[1, g]

    def passed_on(k):
        up = remote(rows3.at[1, k], rows3.at[0, k], side_send.at[0], side_recv.at[0], (d + 1, g))
        down = remote(rows3.at[1, k], rows3.at[2, k], side_send.at[1], side_recv.at[1], (d - 1, g))
        return up, down

    forwards = [passed_on(behind[m]) for m in range(n)] + [passed_on(g)]

    def forward(m):
        up, down = forwards[m]
        @pl.when(d < n_dom - 1)
        def _():
            up.start()
        @pl.when(d > 0)
        def _():
            down.start()

    forward(n)
    for q in range(slots // LANES):
        picked[q * LANES : (q + 1) * LANES, :] = picks(column(owner[0:1, q * LANES : (q + 1) * LANES]), row_nodes)
    base[...] = dot(first[...], weights[7])
    for m in range(n):
        remote(rows3.at[1, behind[m]], rows3.at[1, behind[m]], ag_send, ag_recv.at[m], (d, ahead[m])).wait_recv()
        forward(m)
    senders = dot(picked_senders[:, row_nodes : 2 * row_nodes], rows3[1].reshape(row_nodes, 2 * L))
    receiver = dot(mine, weights[1])
    own_part = dot(mine, weights[4])
    @pl.when(d > 0)
    def _():
        all_of(rows3.at[0], side_recv.at[0])
    @pl.when(d < n_dom - 1)
    def _():
        all_of(rows3.at[2], side_recv.at[1])
    senders = senders + dot(picked_senders[:, :row_nodes], rows3[0].reshape(row_nodes, 2 * L))
    senders = senders + dot(picked_senders[:, 2 * row_nodes :], rows3[2].reshape(row_nodes, 2 * L))
    hidden = swish_pair(dot(senders.astype(BF16), weights[0]) + jnp.concatenate([receiver] * fan, 0))
    message = hidden[:own].astype(F32)
    for j in range(1, fan):
        message = message + hidden[j * own : (j + 1) * own].astype(F32)
    hidden = swish_pair(own_part + dot(message.astype(BF16), weights[5]))
    up, up_tan = norm_pair_lanes(dot(hidden, weights[6]))
    updated[g] = jnp.concatenate([up.astype(BF16), up_tan.astype(BF16)], 1)
    fin = [remote(updated.at[g], updated.at[g], fin_send, fin_recv, (d, ahead[m])) for m in range(n)]
    for m in reversed(range(n)):
        fin[m].start()

    for b, (there, _) in enumerate(sides):
        @pl.when(there)
        def _():
            halo_copies[b].wait_send()
    all_of(arrived, rs_send)
    all_of(arrived, ag_send)
    @pl.when(d < n_dom - 1)
    def _():
        all_of(rows3.at[0], side_send.at[0])
    @pl.when(d > 0)
    def _():
        all_of(rows3.at[2], side_send.at[1])
    all_of(arrived, fin_recv)
    brought = dot(updated[...].reshape(row_nodes, 2 * L), weights[8]).astype(BF16)
    hidden = swish_pair(base[...] + dot(picked[...], brought))
    up, up_tan = norm_pair_lanes(dot(hidden, weights[9]))
    valid = lax.broadcasted_iota(I32, (slots, L), 0) < node_count
    node_output[...] = jnp.where(valid, first[:, :L].astype(F32) + up, 0.0).astype(BF16)
    tangent_output[...] = jnp.where(valid, first[:, L:].astype(F32) + up_tan, 0.0).astype(BF16)
    all_of(arrived, fin_send)


def store_kernel(primal, tan, node_output, tangent_output, sems):
    copies = [pltpu.make_async_copy(primal, node_output, sems.at[0]), pltpu.make_async_copy(tan, tangent_output, sems.at[1])]
    for copy in copies:
        copy.start()
    for copy in copies:
        copy.wait()


def per_device(sizes, *args):
    n_dom, n_grp, ny, nx = sizes
    named = dict(zip(NAMES[:3] + ("node_counts", "edge_counts") + NAMES[3:], args))
    named["coarse_source"] = named["coarse_source"].T
    counts = [named.pop(name) for name in ("node_counts", "edge_counts")]
    shape = {name: a.shape for name, a in named.items()}
    slots, edge_slots, rim = shape["node_latent"][0], shape["edge_latent"][0], shape["send_lists"][2]
    fan, own = shape["coarse_source"]
    row_nodes = n_grp * own
    others = n_grp - 1
    dma = pltpu.SemaphoreType.DMA
    vmem = pltpu.VMEM
    out = jax.ShapeDtypeStruct((slots, L), BF16)
    results = pl.pallas_call(
        functools.partial(layer_kernel, sizes),
        out_shape=(out, out),
        in_specs=[pl.BlockSpec(memory_space=pltpu.SMEM)] * 2 + [pl.BlockSpec(memory_space=pltpu.HBM)] * 18,
        out_specs=(pl.BlockSpec(memory_space=vmem),) * 2,
        scratch_shapes=[vmem((slots, 2 * L), BF16), vmem((edge_slots, L), BF16)]
        + [vmem(shape[name], I32) for name in NAMES[3:8]]
        + [vmem(shape[name], BF16) for name in NAMES[8:]]
        + [
            vmem((4, rim, 2 * L), BF16),
            vmem((4, rim, 2 * L), BF16),
            vmem((2 * slots + 4 * rim, 2 * L), BF16),
            vmem((edge_slots // 2, LANES), I16),
            vmem((edge_slots, 2 * L), F32),
            vmem((edge_slots, 2 * L), BF16),
            vmem((slots, row_nodes), BF16),
            vmem((fan * own, 3 * row_nodes), BF16),
            vmem((slots, 2 * L), F32),
            vmem((11, 2 * L, 2 * L), BF16),
            vmem((2, n_grp, own // 2, 2 * L), BF16),
            vmem((2, others, own // 2, 2 * L), BF16),
            vmem((3, n_grp, own, 2 * L), BF16),
            vmem((n_grp, own, 2 * L), BF16),
            vmem((LANES, LANES), I32),
            vmem((slots, 2 * L), BF16),
            vmem((row_nodes, slots), BF16),
            vmem((4 * rim, slots), BF16),
            dma((4,)), dma((4,)), dma((4,)), dma(()), dma((2,)), dma(()), dma((others,)), dma((2,)), dma((2,)), dma(()), dma(()),
        ],
        compiler_params=pltpu.CompilerParams(collective_id=0, has_side_effects=True, vmem_limit_bytes=VMEM_LIMIT << 20),
    )(*counts, *[pltpu.with_memory_space_constraint(a, pltpu.HBM) for a in named.values()])
    return pl.pallas_call(
        store_kernel,
        out_shape=(out, out),
        in_specs=[pl.BlockSpec(memory_space=pl.ANY)] * 2,
        out_specs=(pl.BlockSpec(memory_space=pltpu.HBM),) * 2,
        scratch_shapes=[dma((2,))],
    )(*[pltpu.with_memory_space_constraint(a, pltpu.VMEM) for a in results])


VMEM_LIMIT = 40


def solution(mesh):
    n_dom, n_grp = mesh.shape["dom"], mesh.shape["grp"]
    nx = 4 if n_grp % 4 == 0 and n_grp > 4 else 2
    both = ("dom", "grp")
    rows = P(both, None)
    in_specs = (rows, rows, rows, P(both), P(both), P(both, None, None), rows, rows, rows, rows) + (P(),) * 10
    return jax.shard_map(
        functools.partial(per_device, (n_dom, n_grp, n_grp // nx, nx)),
        mesh=mesh, in_specs=in_specs, out_specs=(rows, rows), check_vma=False,
    )
```
